256 devices in a mesh: dp: 4 (over x), table: 64 (over y, z, core).
Axes of the slice: x: 4, y: 4, z: 8, core: 2. Of those that a mesh axis runs over, the one named last changes fastest.
Arguments:
- shard_of: int32 [2048, 200, 3], P(('dp', 'table')), may hold values from 0 to 63, all different within a row; in each aligned block of 1600 rows (0 to 1599, 1600 to 3199, ..., all dimensions but the last counted through in order) at most 152 rows name the same one
- offsets: int32 [2048, 200, 3], P(('dp', 'table')), may hold values from 0 to 2047
- table: bfloat16 [3, 131072, 256], P(None, 'table'), may hold values from -4 to 4
- weight_one: bfloat16 [768, 256], replicated, may hold values from -0.21875 to 0.21875
- gain_one: float32 [256], replicated, may hold values from 0.5 to 1.5
- weight_two: bfloat16 [768, 256], replicated, may hold values from -0.21875 to 0.21875
- gain_two: float32 [256], replicated, may hold values from 0.5 to 1.5
- grad_out: bfloat16 [2048, 200, 256], P(('dp', 'table')), may hold values from -6 to 6
Outputs:
- block_out: bfloat16 [2048, 200, 256], P(('dp', 'table'))
- grad_weight_one: float32 [768, 256], replicated
- grad_weight_two: float32 [768, 256], replicated
- grad_gain_one: float32 [256], replicated
- grad_gain_two: float32 [256], replicated
- table_grad: float32 [3, 131072, 256], P(None, 'table', 'dp')
The draws below stay inside these ranges and needn't reach their ends.
Inputs may be any that keep to these rules, and one draw needn't show every extreme that they name: `shard_of`: the three lookups of one item go to three different shards; at most 152 lookups of the items of one device go to one shard, and exactly 152 for some shard of some device.
All inputs are finite; a program needn't handle non-finite values.
Results may differ from the reference program's by a relative error of at most 0.017.
Values may be sent and summed in bfloat16 or wider, within the bound.
A program may use at most 128 MiB of HBM per device.

```python
import math
import jax
import jax.numpy as jnp
import numpy as np
from jax import lax

D = 256
LEN = 200
ROWS_DEV = 2048
SESS_DEV = 8
ITEMS_DEV = 1600
CAP = 152
SESS = 2048
HROWS = 131072
N_TABLE = 64


def touch_ends(values, key, low, high):
    longest = values.shape.index(max(values.shape))
    spots = []
    for shift in (0, 1):
        where = [jax.random.randint(jax.random.fold_in(key, axis), (), 0, length) for axis, length in enumerate(values.shape)]
        where[longest] = (where[longest] + shift) % values.shape[longest]
        spots.append(tuple(where))
    return values.at[spots[0]].set(low).at[spots[1]].set(high)


def block_levels(stream_key, shape, pieces, least, largest):
    factor_of, own = 1.0, jax.random.fold_in(stream_key, 6)
    for axis_at, blocks in pieces:
        steps = jnp.exp(jax.random.uniform(jax.random.fold_in(own, axis_at), (blocks,), jnp.float32, least / len(pieces), largest / len(pieces)))
        factor_of = factor_of * jnp.repeat(steps, shape[axis_at] // blocks).reshape([-1 if axis == axis_at else 1 for axis in range(len(shape))])
    return factor_of


def deal_out(rng, own, number, rows, number_of, top, most, skew):
    ranking = jax.random.permutation(rng, number_of)
    crowded, common = load_shares(number_of, rows * top, most, skew, True), load_shares(number_of, rows * top, most, skew, False)
    places = jnp.arange(number_of)

    def named(sizes, offset_by):
        used = int((sizes > 0).sum())
        fixed = max(1, used // 4)
        moved = fixed + (places - fixed + offset_by * (used - fixed)) % max(1, number_of - fixed)
        return jnp.zeros((number_of,), jnp.int32).at[ranking[jnp.where(places < fixed, places, moved)]].set(jnp.asarray(sizes, jnp.int32))

    sizes = jnp.where(number % 4 == 0, named(crowded, number // 4), named(common, number - number // 4 - 1))
    mixed = jax.random.permutation(jax.random.fold_in(own, 3), number_of)
    donor, sink = mixed[0:number_of // 2 * 2:2], mixed[1:number_of // 2 * 2:2]
    room = jnp.minimum(sizes[donor] - 1, most - sizes[sink]) // 2
    room = jnp.where((donor == ranking[0]) | (sink == ranking[0]) | (sizes[sink] == 0), 0, jnp.maximum(room, 0))
    moved = jax.random.randint(jax.random.fold_in(own, 4), (number_of // 2,), 0, 1 << 20) % (room + 1)
    sizes = sizes.at[donor].add(-moved).at[sink].add(moved)
    items = jnp.searchsorted(jnp.cumsum(sizes), jnp.arange(rows * top), side="right").astype(jnp.int32)
    listing = items.reshape(top, rows).T
    listing = listing[jax.random.permutation(jax.random.fold_in(own, 1), rows)]
    offset_by = jax.random.randint(jax.random.fold_in(own, 2), (rows, 1), 0, top)
    return jnp.take_along_axis(listing, (jnp.arange(top)[None, :] + offset_by) % top, axis=1)


def load_shares(count, total, reach, skew, full):
    portions = [(1 << 20) // math.isqrt(standing ** skew) + 1 for standing in range(1, count + 1)]
    largest = reach if full else min(reach, max(-(-total // count), total * portions[0] // sum(portions)))
    least = 1 if total - largest >= count - 1 else 0
    holding, surplus = [largest] + [least] * (count - 1), total - largest - least * (count - 1)
    while surplus > 0:
        movable = [i for i in range(1, count) if holding[i] < largest] or [i for i in range(1, count) if holding[i] < reach]
        mass, remaining = sum([portions[i] for i in movable]), surplus
        for i in movable:
            extra = min(reach - holding[i], max(1, remaining * portions[i] // mass), surplus)
            holding[i] = holding[i] + extra
            surplus = surplus - extra
    return np.array(holding)


def normal_values(rng, shape, spread, bound, shards=(), held_as=jnp.bfloat16):
    level = block_levels(rng, shape, shards, -0.22, 0.18) if shards else 1.0
    drawn = jax.random.normal(rng, shape, jnp.float32) * spread * level
    return jnp.minimum(jnp.maximum(drawn, -bound), bound).astype(held_as)


def setup_inputs(seed: int = 0) -> dict:
    key_of = jax.random.split(jax.random.key(seed), 9)
    shard_of_keys = jax.random.split(jax.random.fold_in(key_of[0], 1), SESS * LEN // ITEMS_DEV)
    shard_of_turns = jax.random.permutation(jax.random.fold_in(key_of[0], 3), SESS * LEN // ITEMS_DEV)
    shard_of = jax.vmap(lambda own, number: deal_out(jax.random.fold_in(key_of[0], 2), own, number, ITEMS_DEV, N_TABLE, 3, CAP, 2))(shard_of_keys, shard_of_turns).reshape((SESS, LEN, 3))
    offsets = touch_ends(jax.random.randint(key_of[1], (SESS, LEN, 3), 0, ROWS_DEV), jax.random.fold_in(key_of[1], 1), 0, ROWS_DEV - 1).astype(jnp.int32)
    table = normal_values(key_of[2], (3, HROWS, D), 0.6, 4.0, ((1, 64),))
    weight_one = normal_values(key_of[3], (3 * D, D), (3 * D) ** -0.5, 0.21875)
    gain_one = jnp.clip(1.0 + 0.1 * jax.random.normal(key_of[4], (D,), jnp.float32), 0.5, 1.5)
    weight_two = normal_values(key_of[5], (3 * D, D), (3 * D) ** -0.5, 0.21875)
    gain_two = jnp.clip(1.0 + 0.1 * jax.random.normal(key_of[6], (D,), jnp.float32), 0.5, 1.5)
    grad_out = normal_values(key_of[7], (SESS, LEN, D), 1.0, 6.0, ((0, 256),))
    return {"shard_of": shard_of, "offsets": offsets, "table": table, "weight_one": weight_one, "gain_one": gain_one, "weight_two": weight_two, "gain_two": gain_two, "grad_out": grad_out}


GELU_C = 0.7978845608028654
GELU_K = 0.044715

def shifted(values, spacing):
    return jnp.pad(values, ((0, 0), (spacing, 0), (0, 0)))[:, :values.shape[1], :]

def unshifted(values, spacing):
    return jnp.pad(values, ((0, 0), (0, spacing), (0, 0)))[:, spacing:, :]

def stack_taps(values, spacing):
    return jnp.concatenate([values, shifted(values, spacing), shifted(values, 2 * spacing)], axis=-1)

def gelu_parts(inputs):
    inner = GELU_C * (inputs + GELU_K * inputs * inputs * inputs)
    tangent = jnp.tanh(inner)
    output = 0.5 * inputs * (1.0 + tangent)
    slope = 0.5 * (1.0 + tangent) + 0.5 * inputs * (1.0 - tangent * tangent) * GELU_C * (1.0 + 3.0 * GELU_K * inputs * inputs)
    return (output, slope)

def layer_forward(values, weight, gain, spacing):
    sessions, length, width = values.shape
    stacked = stack_taps(values, spacing).reshape(sessions * length, 3 * width)
    before_norm = jnp.dot(stacked, weight, preferred_element_type=jnp.float32)
    centred = before_norm - lax.optimization_barrier(jnp.mean(before_norm, axis=-1, keepdims=True))
    inv_std = lax.rsqrt(lax.optimization_barrier(jnp.mean(centred * centred, axis=-1, keepdims=True)) + 1e-05)
    normal = centred * inv_std
    output, slope = gelu_parts(normal * gain)
    return (output, (stacked, normal, inv_std, slope))

def layer_backward(grad_output, weight, gain, saved, spacing, sessions, length):
    stacked, normal, inv_std, slope = saved
    width = weight.shape[1]
    grad_scaled = grad_output * slope
    grad_gain = lax.optimization_barrier(jnp.sum(grad_scaled * normal, axis=0))
    grad_normal = grad_scaled * gain
    grad_before = inv_std * (grad_normal - lax.optimization_barrier(jnp.mean(grad_normal, axis=-1, keepdims=True)) - normal * lax.optimization_barrier(jnp.mean(grad_normal * normal, axis=-1, keepdims=True)))
    grad_before = grad_before.astype(jnp.bfloat16)
    grad_weight = lax.dot_general(stacked, grad_before, (((0,), (0,)), ((), ())), preferred_element_type=jnp.float32)
    grad_taps = lax.dot_general(grad_before, weight, (((1,), (1,)), ((), ())), preferred_element_type=jnp.float32).reshape(sessions, length, 3 * width)
    grad_input = grad_taps[..., :width] + unshifted(grad_taps[..., width:2 * width], spacing) + unshifted(grad_taps[..., 2 * width:], 2 * spacing)
    return (grad_input, grad_weight, grad_gain)

def block_pass(embedded, weight_one, gain_one, weight_two, gain_two, grad_out):
    sessions, length, width = embedded.shape
    item_count = sessions * length
    act_one, saved_one = layer_forward(embedded, weight_one, gain_one, 1)
    hidden = act_one.astype(jnp.bfloat16).reshape(sessions, length, width)
    act_two, saved_two = layer_forward(hidden, weight_two, gain_two, 2)
    block_out = (embedded.reshape(item_count, width).astype(jnp.float32) + act_two).astype(jnp.bfloat16)
    grad_top = grad_out.reshape(item_count, width).astype(jnp.float32)
    grad_hidden, second_weights, second_gains = layer_backward(grad_top, weight_two, gain_two, saved_two, 2, sessions, length)
    grad_inner, first_weights, first_gains = layer_backward(grad_hidden.reshape(item_count, width), weight_one, gain_one, saved_one, 1, sessions, length)
    grad_embed = (grad_top + grad_inner.reshape(item_count, width)).astype(jnp.bfloat16)
    return (block_out, grad_embed, first_weights, second_weights, first_gains, second_gains)

def reference(shard_of, offsets, table, weight_one, gain_one, weight_two, gain_two, grad_out):
    global_rows = (shard_of * ROWS_DEV + offsets).astype(jnp.int32)
    block_count = SESS // SESS_DEV
    rows_blocks = global_rows.reshape(block_count, SESS_DEV, LEN, 3)
    grad_blocks = grad_out.reshape(block_count, SESS_DEV, LEN, D)
    picker = jnp.arange(3, dtype=jnp.int32)[None, None, :]

    def one_block(carry, inputs):
        rows_here, grad_here = inputs
        looked = table[picker, rows_here]
        embedded = lax.optimization_barrier(jnp.sum(looked.astype(jnp.float32), axis=2)).astype(jnp.bfloat16)
        block_out, grad_embed, first_weights, second_weights, first_gains, second_gains = block_pass(embedded, weight_one, gain_one, weight_two, gain_two, grad_here)
        new_carry = (carry[0] + first_weights, carry[1] + second_weights, carry[2] + first_gains, carry[3] + second_gains)
        return (new_carry, (block_out.reshape(SESS_DEV, LEN, D), grad_embed.reshape(SESS_DEV, LEN, D)))
    start = (jnp.zeros((3 * D, D), jnp.float32), jnp.zeros((3 * D, D), jnp.float32), jnp.zeros((D,), jnp.float32), jnp.zeros((D,), jnp.float32))
    totals, (outputs, grads) = lax.scan(one_block, start, (rows_blocks, grad_blocks))
    scale = 1.0 / math.sqrt(SESS * LEN)
    flat_rows = global_rows.reshape(SESS * LEN, 3)
    flat_grads = grads.reshape(SESS * LEN, D).astype(jnp.float32)
    table_grad = jnp.zeros((3, HROWS, D), jnp.float32)
    for column in range(3):
        table_grad = table_grad.at[column, flat_rows[:, column]].add(flat_grads)
    return (outputs.reshape(SESS, LEN, D), totals[0] * scale, totals[1] * scale, totals[2] * scale, totals[3] * scale, table_grad)
```

```python
import functools
import math

import jax
import jax.numpy as jnp
from jax import lax
from jax.experimental import pallas as pl
from jax.experimental.pallas import tpu as pltpu
from jax.sharding import PartitionSpec as P

F32, BF16, I32 = jnp.float32, jnp.bfloat16, jnp.int32
MESH = pl.DeviceIdType.MESH
GELU_C = 0.7978845608028654
GELU_K = 0.044715
GROUP = 8
AXES = (("dp", 4, 1), ("table", 4, 16), ("table", 8, 2), ("table", 2, 1))


def gelu_parts(inputs):
    inner = GELU_C * (inputs + GELU_K * inputs * inputs * inputs)
    tangent = jnp.tanh(inner)
    output = 0.5 * inputs * (1.0 + tangent)
    slope = 0.5 * (1.0 + tangent) + 0.5 * inputs * (1.0 - tangent * tangent) * GELU_C * (
        1.0 + 3.0 * GELU_K * inputs * inputs
    )
    return (output, slope)


def index_kernel(shards, cap, rows_dev, sh_ref, off_ref, place_ref, req_ref, item_ref):
    tables, sessions, length = sh_ref.shape
    tri = (
        lax.broadcasted_iota(I32, (length, length), 0) < lax.broadcasted_iota(I32, (length, length), 1)
    ).astype(BF16)
    lane = lax.broadcasted_iota(I32, (1, length), 1)
    shard_id = lax.broadcasted_iota(I32, (shards, length), 0)
    slot_id = lax.broadcasted_iota(I32, (cap, length), 0)
    base = jnp.zeros((shards, 1), F32)
    listed = [jnp.zeros((shards, cap), F32) for _ in range(4)]
    dims = (((1,), (1,)), ((), ()))
    for t in range(tables):
        for s in range(sessions):
            sh = sh_ref[t, s : s + 1, :]
            code = off_ref[t, s : s + 1, :] + (t * rows_dev + 1)
            item = lane + s * length
            hit = shard_id == sh
            hot = jnp.where(hit, 1.0, 0.0)
            hot16 = hot.astype(BF16)
            prefix = jnp.dot(hot16, tri, preferred_element_type=F32) + base
            rank = jnp.sum(jnp.where(hit, prefix, 0.0), axis=0, keepdims=True).astype(I32)
            base = base + jnp.sum(hot, axis=1, keepdims=True)
            place_ref[t, s : s + 1, :] = sh * cap + rank
            here = slot_id == rank
            for n, digit in enumerate((code // 256, code % 256, item // 256, item % 256)):
                listed[n] += lax.dot_general(
                    hot16,
                    jnp.where(here, digit.astype(F32), 0.0).astype(BF16),
                    dims,
                    preferred_element_type=F32,
                )
    req_ref[...] = (listed[0] * 256.0 + listed[1]).astype(I32)
    item_ref[...] = (listed[2] * 256.0 + listed[3]).astype(I32)


def make_index(sh, off, shards, cap, rows_dev):
    block = jax.ShapeDtypeStruct((shards, cap), I32)
    return pl.pallas_call(
        functools.partial(index_kernel, shards, cap, rows_dev),
        out_shape=(jax.ShapeDtypeStruct(sh.shape, I32), block, block),
        cost_estimate=pl.CostEstimate(flops=10**9, bytes_accessed=10**6, transcendentals=0),
        name="index",
    )(sh, off)


def whole(shape):
    zeros = (0,) * len(shape)
    return pl.BlockSpec(shape, lambda b, i: zeros, pipeline_mode=pl.Buffered(1))


def widen(src, dst, rows, at=0):
    values = src[pl.ds(at, rows), :].astype(F32)
    dst[pl.ds(2 * at, rows, stride=2), :] = values[:, :128]
    dst[pl.ds(2 * at + 1, rows, stride=2), :] = values[:, 128:]


def pair(index):
    return pl.ds(pl.multiple_of(2 * index, 2), 2)


PAD = 8


def padded(values, length):
    zeros = jnp.zeros((PAD, values.shape[1]), F32)
    parts = []
    for start in range(0, values.shape[0], length):
        parts += [zeros, values[start : start + length]]
    return jnp.concatenate(parts, axis=0)


def unpadded(values, length):
    pitch = length + PAD
    return jnp.concatenate(
        [values[start + PAD : start + pitch] for start in range(0, values.shape[0], pitch)], axis=0
    )


def rolled(values, by):
    return [values.astype(BF16)] + [
        pltpu.roll(values, (k * by) % values.shape[0], 0).astype(BF16) for k in (1, 2)
    ]


def normalized(before):
    centred = before - jnp.mean(before, axis=-1, keepdims=True)
    inv_std = lax.rsqrt(jnp.mean(centred * centred, axis=-1, keepdims=True) + 1e-05)
    return centred * inv_std, inv_std


def forward(values, weight_ref, gain, spacing):
    width = values.shape[1]
    before = jnp.zeros(values.shape, F32)
    for k, tap in enumerate(rolled(values, spacing)):
        before += jnp.dot(tap, weight_ref[k * width : (k + 1) * width, :], preferred_element_type=F32)
    normal, inv_std = normalized(before)
    output, slope = gelu_parts(normal * gain)
    return output, normal, inv_std, slope


def backward(grad_output, values, saved, weight_ref, gain, spacing, weight_grad_ref):
    normal, inv_std, slope = saved
    width = values.shape[1]
    scaled = grad_output * slope
    gain_grad = jnp.sum(scaled * normal, axis=0, keepdims=True)
    back = scaled * gain
    before = inv_std * (
        back
        - jnp.mean(back, axis=-1, keepdims=True)
        - normal * jnp.mean(back * normal, axis=-1, keepdims=True)
    )
    grad_input = jnp.zeros(values.shape, F32)
    taken = values.astype(BF16)
    for k, tap in enumerate(rolled(before, -spacing)):
        rows = slice(k * width, (k + 1) * width)
        grad_input += lax.dot_general(
            tap, weight_ref[rows, :], (((1,), (1,)), ((), ())), preferred_element_type=F32
        )
        weight_grad_ref[rows, :] += lax.dot_general(
            taken, tap, (((0,), (0,)), ((), ())), preferred_element_type=F32
        )
    return grad_input, gain_grad


def block_kernel(
    length, place_ref, got_ref, w1_ref, g1_ref, w2_ref, g2_ref, top_ref,
    out_ref, grad_ref, dw1_ref, dw2_ref, gains_ref, wide, total,
):
    items, width = out_ref.shape
    slots = got_ref.shape[0]
    step = slots // 16

    @pl.loop(0, 16)
    def _(c):
        widen(got_ref, wide, step, pl.multiple_of(c * step, 16))

    @pl.loop(0, items // 16)
    def _(g):
        at = pl.multiple_of(g * 16, 16)
        for k in range(16):
            a, b, c = [wide[pair(place_ref[t * items + at + k]), :] for t in range(3)]
            total[pl.ds(2 * at + 2 * k, 2), :] = a + b + c

    dw1_ref[...] = jnp.zeros(dw1_ref.shape, F32)
    dw2_ref[...] = jnp.zeros(dw2_ref.shape, F32)
    gains_ref[...] = jnp.zeros(gains_ref.shape, F32)
    chunk = 2 * length
    pitch = length + PAD
    row = lax.broadcasted_iota(I32, (2 * pitch, width), 0)
    real = ((row >= PAD) & (row < pitch)) | (row >= pitch + PAD)
    g1, g2 = g1_ref[...], g2_ref[...]

    @pl.loop(0, items // chunk)
    def _(c):
        at = pl.ds(pl.multiple_of(c * chunk, 16), chunk)
        embedded = jnp.concatenate(
            [total[pl.ds(2 * c * chunk + h, chunk, stride=2), :] for h in range(2)], axis=1
        )
        embedded = padded(embedded.astype(BF16).astype(F32), length)
        act_one, *saved_one = forward(embedded, w1_ref, g1, 1)
        hidden = jnp.where(real, act_one, 0.0).astype(BF16).astype(F32)
        act_two, *saved_two = forward(hidden, w2_ref, g2, 2)
        out_ref[at, :] = unpadded(embedded + act_two, length).astype(BF16)
        top = padded(top_ref[at, :].astype(F32), length)
        grad_hidden, gain_two = backward(top, hidden, saved_two, w2_ref, g2, 2, dw2_ref)
        grad_hidden = jnp.where(real, grad_hidden, 0.0)
        grad_inner, gain_one = backward(grad_hidden, embedded, saved_one, w1_ref, g1, 1, dw1_ref)
        grad_ref[at, :] = unpadded(top + grad_inner, length).astype(BF16)
        gains_ref[0:1, :] += gain_one
        gains_ref[1:2, :] += gain_two


def block_pass(place, got, length, weight_one, gain_one, weight_two, gain_two, grad_top):
    items, width = grad_top.shape
    operands = (got, weight_one, gain_one.reshape(1, -1), weight_two, gain_two.reshape(1, -1), grad_top)
    shapes = [
        ((items, width), BF16),
        ((items, width), BF16),
        (weight_one.shape, F32),
        (weight_two.shape, F32),
        ((8, width), F32),
    ]
    return pl.pallas_call(
        functools.partial(block_kernel, length),
        out_shape=[jax.ShapeDtypeStruct(*shape) for shape in shapes],
        grid_spec=pltpu.PrefetchScalarGridSpec(
            num_scalar_prefetch=1,
            grid=(1,),
            in_specs=[whole(operand.shape) for operand in operands],
            out_specs=[whole(shape) for shape, _ in shapes],
            scratch_shapes=[pltpu.VMEM((2 * got.shape[0], 128), F32), pltpu.VMEM((2 * items, 128), F32)],
        ),
        cost_estimate=pl.CostEstimate(flops=4 * 10**9, bytes_accessed=30 * 10**6, transcendentals=10**6),
        name="block_pass",
    )(place, *operands)


def collect_kernel(ways, idx_ref, got_ref, out_ref, wide, *accs):
    b = pl.program_id(0)
    block = got_ref.shape[0]
    rows = accs[0].shape[0] // 2 - 8
    unroll = 32

    @pl.when(b == 0)
    def _():
        @pl.loop(0, rows // 256)
        def _(c):
            for acc in accs:
                acc[pl.ds(pl.multiple_of(c * 512, 512), 512), :] = jnp.zeros((512, 128), F32)

    widen(got_ref, wide, block)

    @pl.loop(0, block // unroll)
    def _(g):
        at = pl.multiple_of(g * (2 * unroll), 2 * unroll)
        spots = [pair(idx_ref[b * block + g * unroll + k]) for k in range(unroll)]
        for k in range(0, unroll, ways):
            olds = [accs[j][spots[k + j], :] for j in range(ways)]
            adds = [wide[pl.ds(at + 2 * (k + j), 2), :] for j in range(ways)]
            for j in range(ways):
                accs[j][spots[k + j], :] = olds[j] + adds[j]

    @pl.when(b == pl.num_programs(0) - 1)
    def _():
        @pl.loop(0, rows // 256)
        def _(c):
            per = out_ref.shape[2] // 256
            to = pl.ds(pl.multiple_of((c % per) * 256, 256), 256)
            for half in range(2):
                at = pl.ds(c * 512 + half, 256, stride=2)
                total = accs[0][at, :]
                for acc in accs[1:]:
                    total = total + acc[at, :]
                out_ref[c // per, 128 * half : 128 * half + 128, to] = total.T.astype(BF16)


def collect(idx, got, rows, block=2432, ways=4):
    n, width = got.shape
    shape = (3, width, rows // 3)
    return pl.pallas_call(
        functools.partial(collect_kernel, ways),
        out_shape=jax.ShapeDtypeStruct(shape, BF16),
        grid_spec=pltpu.PrefetchScalarGridSpec(
            num_scalar_prefetch=1,
            grid=(n // block,),
            in_specs=[pl.BlockSpec((block, width), lambda b, i: (b, 0))],
            out_specs=whole(shape),
            scratch_shapes=[pltpu.VMEM((2 * block, 128), F32)]
            + [pltpu.VMEM((2 * (rows + 8), 128), F32)] * ways,
        ),
        cost_estimate=pl.CostEstimate(flops=10**7, bytes_accessed=60 * 10**6, transcendentals=0),
        name="collect",
    )(idx, got)


def peer_of(axis, step):
    name, size, stride = AXES[axis]
    index = lax.axis_index(name)
    mine = lax.rem(lax.div(index, stride), size)
    other = lax.rem(mine + step, size)
    return mine, other, {name: index + (other - mine) * stride}


def visit(step):
    (_, ysize, ystride), (_, zsize, zstride), (_, csize, _) = AXES[1:]
    me = lax.axis_index("table")
    y, z, c = lax.div(me, ystride), lax.rem(lax.div(me, zstride), zsize), lax.rem(me, csize)
    turn = lax.rem(step, zsize)
    half = lax.div(turn + 1, 2)
    away = jnp.where(lax.rem(turn, 2) == 1, half, zsize - half)
    y = lax.rem(y + lax.rem(lax.div(step, zsize), ysize), ysize)
    z = lax.rem(z + away, zsize)
    c = lax.rem(c + lax.div(step, zsize * ysize), csize)
    return y * ystride + z * zstride + c


def remote(src, dst, send, recv, device):
    return pltpu.make_async_remote_copy(
        src_ref=src, dst_ref=dst, send_sem=send, recv_sem=recv, device_id=device, device_id_type=MESH
    )


def exchange_kernel(scale, idx_ref, table_ref, *rest):
    summing = scale is not None
    if summing:
        w1_ref, w2_ref, gains_ref, got_ref, out_ref, wide, stage, held, own_sem, sends, recv, *more = rest
        part, r0, s0, r1, a1, xsend, xrecv, tsend, trecv, gsend, grecv, ysend, yrecv = more
    else:
        got_ref, wide, stage, held, own_sem, sends, recv = rest
    shards, cap, width = held.shape
    rows = table_ref.shape[0]
    me = lax.axis_index("table")
    group = GROUP
    total = shards - 1

    barrier = pltpu.get_barrier_semaphore()

    def hello(step, _):
        pl.semaphore_signal(barrier, inc=1, device_id={"table": visit(step)}, device_id_type=MESH)
        return 0

    lax.fori_loop(1, shards, hello, 0)
    if summing:
        for step in range(1, AXES[0][1]):
            pl.semaphore_signal(barrier, inc=1, device_id=peer_of(0, step)[2], device_id_type=MESH)

    def widened(c, _):
        at = pl.ds(pl.multiple_of(c * 64, 64), 64)
        wide[at, :] = table_ref[at, :].astype(F32)
        return 0

    lax.fori_loop(0, rows // 64, widened, 0)
    if summing:
        n, m = part.shape[1], w1_ref.shape[0]
        part[0] = w1_ref[0:n]
        part[1, 0 : m - n] = w1_ref[n:m]
        part[1, m - n : n] = w2_ref[0 : 2 * n - m]
        part[2] = w2_ref[2 * n - m : m]
        part[3, 0] = gains_ref[...]
        part[3, 1:] = jnp.zeros((n - 1,) + part.shape[2:], F32)

    def gather(step):
        dest = visit(step)
        for k in range(0, cap, 8):
            rows8 = [wide[pl.ds(idx_ref[dest * cap + k + j], 1), :] for j in range(8)]
            stage[k : k + 8, :] = jnp.concatenate(rows8, axis=0)
        held[step] = stage[...].astype(BF16)

    def post(step):
        remote(
            held.at[step],
            got_ref.at[me],
            sends.at[lax.div(step - 1, group)],
            recv,
            {"table": visit(step)},
        ).start()

    def sent(number, count):
        ref = held.at[pl.ds(0, count)]
        remote(ref, ref, sends.at[number], recv, {"table": visit(1)}).wait_send()

    gather(0)
    own = pltpu.make_async_copy(held.at[0], got_ref.at[me], own_sem)
    gather(1)
    pl.semaphore_wait(barrier, total + (AXES[0][1] - 1 if summing else 0))
    own.start()
    if summing:
        xcopies = []
        for step in range(1, AXES[0][1]):
            _, other, device = peer_of(0, step)
            xcopies.append(
                remote(part.at[other], r0.at[step - 1], xsend.at[step - 1], xrecv.at[step - 1], device)
            )
            xcopies[-1].start()
        xmine = peer_of(0, 1)[0]

    def go(step, _):
        gather(step)
        post(step - 1)
        return 0

    groups = -(-total // group)
    for number in range(groups):
        if summing and number >= 2:
            sent(number - 2, group)
        low, high = number * group + 2, min((number + 1) * group + 1, shards - 1)
        lax.fori_loop(low, high + 1, go, 0)
        if number == groups - 1:
            post(shards - 1)
        if summing and number == min(2, groups - 1):
            value = part[xmine]
            for step, copy in enumerate(xcopies):
                copy.wait_recv()
                value = value + r0[step]
            s0[...] = value

            def give(step, _):
                dest = visit(step)
                remote(s0.at[dest], r1.at[me], tsend, trecv, {"table": dest}).start()
                return 0

            r1[me] = s0[me]
            lax.fori_loop(1, shards, give, 0)
        if summing and number == min(4, groups - 1):
            many = s0.at[pl.ds(0, total)]
            remote(many, r1.at[pl.ds(0, total)], tsend, trecv, {"table": visit(1)}).wait_recv()
            a1[me] = lax.fori_loop(0, shards, lambda t, v: v + r1[t], jnp.zeros(a1.shape[1:], F32)) * scale

            def show(step, _):
                remote(a1.at[me], a1.at[me], gsend, grecv, {"table": visit(step)}).start()
                return 0

            lax.fori_loop(1, shards, show, 0)
        if summing and number == min(6, groups - 1):
            many = a1.at[pl.ds(0, total)]
            remote(many, many, gsend, grecv, {"table": visit(1)}).wait_recv()
            ycopies = []
            for step in range(1, AXES[0][1]):
                copy = remote(a1, out_ref.at[xmine], ysend.at[step - 1], yrecv.at[step - 1], peer_of(0, step)[2])
                copy.start()
                ycopies.append(copy)
            out_ref[xmine] = a1[...]
    for number in range(groups):
        if not summing or number >= groups - 2:
            sent(number, min(group, total - number * group))
    own.wait()
    ref = held.at[pl.ds(0, total)]
    remote(ref, got_ref.at[pl.ds(0, total)], sends.at[0], recv, {"table": visit(1)}).wait_recv()
    if summing:
        for copy in xcopies:
            copy.wait_send()
        many = a1.at[pl.ds(0, total)]
        remote(many, many, tsend, trecv, {"table": visit(1)}).wait_send()
        remote(many, many, gsend, grecv, {"table": visit(1)}).wait_send()
        for copy in ycopies:
            copy.wait()


def exchange(idx, table, shards, collective_id, name, sums=None):
    (rows, width), cap = table.shape, idx.shape[0] // shards
    any_space, vmem = pl.BlockSpec(memory_space=pl.ANY), pl.BlockSpec(memory_space=pltpu.VMEM)
    out_shape = [jax.ShapeDtypeStruct((shards, cap, width), BF16)]
    out_specs = [any_space]
    scratch = [
        pltpu.VMEM((rows, width), F32),
        pltpu.VMEM((cap, width), F32),
        pltpu.VMEM((shards, cap, width), BF16),
        pltpu.SemaphoreType.DMA,
        pltpu.SemaphoreType.DMA((-(-(shards - 1) // GROUP),)),
        pltpu.SemaphoreType.DMA,
    ]
    operands, scale = [], None
    if sums is not None:
        *operands, scale = sums
        xsize = AXES[0][1]
        tile = operands[0].shape[1:]
        out_shape.append(jax.ShapeDtypeStruct((xsize, shards) + tile, F32))
        out_specs.append(vmem)
        block = (shards,) + tile
        scratch += [
            pltpu.VMEM((xsize,) + block, F32),
            pltpu.VMEM((xsize - 1,) + block, F32),
            pltpu.VMEM(block, F32),
            pltpu.VMEM(block, F32),
            pltpu.VMEM(block, F32),
        ]
        several, one = pltpu.SemaphoreType.DMA((xsize - 1,)), pltpu.SemaphoreType.DMA
        scratch += [several, several, one, one, one, one, several, several]
    return pl.pallas_call(
        functools.partial(exchange_kernel, scale),
        out_shape=out_shape,
        in_specs=[pl.BlockSpec(memory_space=pltpu.SMEM)] + [vmem] * (1 + len(operands)),
        out_specs=out_specs,
        scratch_shapes=scratch,
        compiler_params=pltpu.CompilerParams(collective_id=collective_id, has_side_effects=True),
        cost_estimate=pl.CostEstimate(flops=10**7, bytes_accessed=10**8, transcendentals=0),
        name=name,
    )(idx, table, *operands)


def greet(steps):
    barrier = pltpu.get_barrier_semaphore()
    for axis, step in steps:
        pl.semaphore_signal(barrier, inc=1, device_id=peer_of(axis, step)[2], device_id_type=MESH)
    pl.semaphore_wait(barrier, len(steps))


def group_sum_kernel(dense_ref, out_ref, own, land, local, send, recv):
    tables, quarter, _ = out_ref.shape
    greet([(0, step) for step in range(1, 4)])
    copies = []
    for t in range(tables):
        for step in range(1, 4):
            mine, other, device = peer_of(0, step)
            copy = pltpu.make_async_remote_copy(
                src_ref=dense_ref.at[t, pl.ds(pl.multiple_of(other * quarter, quarter), quarter)],
                dst_ref=land.at[t, step - 1],
                send_sem=send.at[3 * t + step - 1],
                recv_sem=recv.at[3 * t + step - 1],
                device_id=device,
                device_id_type=MESH,
            )
            copy.start()
            copies.append(copy)
    mine = peer_of(0, 1)[0]
    mine_at = pl.ds(pl.multiple_of(mine * quarter, quarter), quarter)
    kept = [pltpu.make_async_copy(dense_ref.at[t, mine_at], own.at[t], local.at[t]) for t in range(tables)]
    for copy in kept:
        copy.start()
    for t in range(tables):
        kept[t].wait()
        for step in range(3):
            copies[3 * t + step].wait_recv()
        total = own[t].astype(F32)
        for step in range(3):
            total = total + land[t, step].astype(F32)
        out_ref[t] = total
    for copy in copies:
        copy.wait_send()


def group_sum(dense):
    tables, width, rows = dense.shape
    quarter = width // 4
    return pl.pallas_call(
        group_sum_kernel,
        out_shape=jax.ShapeDtypeStruct((tables, quarter, rows), F32),
        in_specs=[pl.BlockSpec(memory_space=pl.ANY)],
        out_specs=pl.BlockSpec(memory_space=pltpu.VMEM),
        scratch_shapes=[
            pltpu.VMEM((tables, quarter, rows), BF16),
            pltpu.VMEM((tables, 3, quarter, rows), BF16),
            pltpu.SemaphoreType.DMA((tables,)),
            pltpu.SemaphoreType.DMA((3 * tables,)),
            pltpu.SemaphoreType.DMA((3 * tables,)),
        ],
        compiler_params=pltpu.CompilerParams(collective_id=2, has_side_effects=True),
        cost_estimate=pl.CostEstimate(flops=10**6, bytes_accessed=60 * 10**6, transcendentals=0),
        name="group_sum",
    )(dense)


def on_device(shard_of, offsets, table, weight_one, gain_one, weight_two, gain_two, grad_out):
    sessions, length, _ = shard_of.shape
    width = table.shape[2]
    rows_dev = table.shape[1]
    rows = 3 * rows_dev
    item_count = sessions * length
    shards = lax.axis_size("table")
    groups = lax.axis_size("dp")
    slot_count = 8 * ((6 * item_count + 8 * shards - 1) // (8 * shards))
    place, requests, items = make_index(
        jnp.transpose(shard_of, (2, 0, 1)), jnp.transpose(offsets, (2, 0, 1)), shards, slot_count, rows_dev
    )
    asked = lax.all_to_all(requests, "table", split_axis=0, concat_axis=0, tiled=True).reshape(-1)
    found = jnp.maximum(asked - 1, 0)
    spots = jnp.where(asked > 0, asked - 1, rows)
    (got,) = exchange(found, table.reshape(rows, width), shards, 0, "rows_out")
    scale = 1.0 / math.sqrt(item_count * groups * shards)
    block_out, grad_embed, first_weights, second_weights, gains = block_pass(
        place.reshape(-1),
        got.reshape(-1, width),
        length,
        weight_one,
        gain_one,
        weight_two,
        gain_two,
        grad_out.reshape(item_count, width),
    )
    tiles = (-1, 8, width)
    arrived, totals = exchange(
        items.reshape(-1),
        grad_embed,
        shards,
        1,
        "grads_out",
        (first_weights.reshape(tiles), second_weights.reshape(tiles), gains, scale),
    )
    totals = totals.reshape(-1, width)
    dense = collect(spots, arrived.reshape(-1, width), rows)
    table_grad = jnp.transpose(group_sum(dense), (0, 2, 1))
    block_out = block_out.reshape(sessions, length, width)
    return block_out, totals[:768], totals[768:1536], totals[1536], totals[1537], table_grad


def solution(mesh):
    placed = (
        P(("dp", "table"), None, None),
        P(("dp", "table"), None, None),
        P(None, "table", None),
        P(),
        P(),
        P(),
        P(),
        P(("dp", "table"), None, None),
    )
    return jax.shard_map(
        on_device,
        mesh=mesh,
        in_specs=placed,
        out_specs=(P(("dp", "table"), None, None), P(), P(), P(), P(), P(None, "table", "dp")),
        check_vma=False,
    )
```

```python
import functools
import math

import jax
import jax.numpy as jnp
from jax import lax
from jax.experimental import pallas as pl
from jax.experimental.pallas import tpu as pltpu
from jax.sharding import PartitionSpec as P

F32, BF16, I32 = jnp.float32, jnp.bfloat16, jnp.int32
MESH = pl.DeviceIdType.MESH
GELU_C = 0.7978845608028654
GELU_K = 0.044715
PITCH = 256
EDGE = 8
GROUP = 8
AXES = (("dp", 4, 1), ("table", 4, 16), ("table", 8, 2), ("table", 2, 1))


def gelu_parts(inputs):
    inner = GELU_C * (inputs + GELU_K * inputs * inputs * inputs)
    tangent = jnp.tanh(inner)
    output = 0.5 * inputs * (1.0 + tangent)
    slope = 0.5 * (1.0 + tangent) + 0.5 * inputs * (1.0 - tangent * tangent) * GELU_C * (
        1.0 + 3.0 * GELU_K * inputs * inputs
    )
    return (output, slope)


def index_kernel(cap, rows_dev, sh_ref, off_ref, place_ref, asked_ref, item_ref, req_ref, send, recv):
    tables, sessions, length = sh_ref.shape
    shards = asked_ref.shape[0]
    me = lax.axis_index("table")
    barrier = pltpu.get_barrier_semaphore()

    def hello(step, _):
        pl.semaphore_signal(barrier, inc=1, device_id={"table": visit(step)}, device_id_type=MESH)
        return 0

    lax.fori_loop(1, shards, hello, 0)
    tri = (
        lax.broadcasted_iota(I32, (length, length), 0) < lax.broadcasted_iota(I32, (length, length), 1)
    ).astype(BF16)
    lane = lax.broadcasted_iota(I32, (1, length), 1)
    shard_id = lax.broadcasted_iota(I32, (shards, length), 0)
    slot_id = lax.broadcasted_iota(I32, (cap, length), 0)
    base = jnp.zeros((shards, 1), F32)
    listed = [jnp.zeros((shards, cap), F32) for _ in range(4)]
    dims = (((1,), (1,)), ((), ()))
    for t in range(tables):
        for s in range(sessions):
            sh = sh_ref[t, s : s + 1, :]
            code = off_ref[t, s : s + 1, :] + (t * rows_dev + EDGE)
            item = lane + (s * length + EDGE)
            hit = shard_id == sh
            hot = jnp.where(hit, 1.0, 0.0)
            hot16 = hot.astype(BF16)
            prefix = jnp.dot(hot16, tri, preferred_element_type=F32) + base
            rank = jnp.sum(jnp.where(hit, prefix, 0.0), axis=0, keepdims=True).astype(I32)
            base = base + jnp.sum(hot, axis=1, keepdims=True)
            place = sh * cap + rank
            place_ref[t * sessions + s, 0:1, :] = place[:, :128]
            place_ref[t * sessions + s, 1:2, 0 : length - 128] = place[:, 128:]
            here = slot_id == rank
            for n, digit in enumerate((code // 256, code % 256, item // 256, item % 256)):
                listed[n] += lax.dot_general(
                    hot16,
                    jnp.where(here, digit.astype(F32), 0.0).astype(BF16),
                    dims,
                    preferred_element_type=F32,
                )
    for ref, high, low in ((req_ref, listed[0], listed[1]), (item_ref, listed[2], listed[3])):
        codes = (high * 256.0 + low).astype(I32)
        ref[...] = jnp.zeros(ref.shape, I32)
        ref[:, 0, :] = codes[:, :128]
        ref[:, 1, 0 : cap - 128] = codes[:, 128:]
    pl.semaphore_wait(barrier, shards - 1)

    def ask(step, _):
        dest = visit(step)
        remote(req_ref.at[dest], asked_ref.at[me], send, recv, {"table": dest}).start()
        return 0

    lax.fori_loop(1, shards, ask, 0)
    asked_ref[me] = req_ref[me]
    many = pl.ds(0, shards - 1)
    remote(req_ref.at[many], asked_ref.at[many], send, recv, {"table": visit(1)}).wait()


def make_index(sh, off, shards, cap, rows_dev):
    tables, sessions, _ = sh.shape
    block = jax.ShapeDtypeStruct((shards, 2, 128), I32)
    vmem = pl.BlockSpec(memory_space=pltpu.VMEM)
    return pl.pallas_call(
        functools.partial(index_kernel, cap, rows_dev),
        out_shape=(jax.ShapeDtypeStruct((tables * sessions, 2, 128), I32), block, block),
        in_specs=[vmem] * 2,
        out_specs=[vmem] * 3,
        scratch_shapes=[pltpu.VMEM((shards, 2, 128), I32), pltpu.SemaphoreType.DMA, pltpu.SemaphoreType.DMA],
        compiler_params=pltpu.CompilerParams(collective_id=3, has_side_effects=True),
        cost_estimate=pl.CostEstimate(flops=10**9, bytes_accessed=10**6, transcendentals=0),
        name="index",
    )(sh, off)


def whole(shape):
    zeros = (0,) * len(shape)
    return pl.BlockSpec(shape, lambda b, i: zeros, pipeline_mode=pl.Buffered(1))


def widen(src, dst, rows, at=0):
    values = src[pl.ds(at, rows), :].astype(F32)
    dst[pl.ds(2 * at, rows, stride=2), :] = values[:, :128]
    dst[pl.ds(2 * at + 1, rows, stride=2), :] = values[:, 128:]


def pair(index):
    return pl.ds(pl.multiple_of(2 * index, 2), 2)


PAD = 8


def padded(values, length):
    zeros = jnp.zeros((PAD, values.shape[1]), F32)
    parts = []
    for start in range(0, values.shape[0], length):
        parts += [zeros, values[start : start + length]]
    return jnp.concatenate(parts, axis=0)


def unpadded(values, length):
    pitch = length + PAD
    return jnp.concatenate(
        [values[start + PAD : start + pitch] for start in range(0, values.shape[0], pitch)], axis=0
    )


def rolled(values, by):
    return [values.astype(BF16)] + [
        pltpu.roll(values, (k * by) % values.shape[0], 0).astype(BF16) for k in (1, 2)
    ]


def normalized(before):
    centred = before - jnp.mean(before, axis=-1, keepdims=True)
    inv_std = lax.rsqrt(jnp.mean(centred * centred, axis=-1, keepdims=True) + 1e-05)
    return centred * inv_std, inv_std


def forward(values, weight_ref, gain, spacing):
    width = values.shape[1]
    before = jnp.zeros(values.shape, F32)
    for k, tap in enumerate(rolled(values, spacing)):
        before += jnp.dot(tap, weight_ref[k * width : (k + 1) * width, :], preferred_element_type=F32)
    normal, inv_std = normalized(before)
    output, slope = gelu_parts(normal * gain)
    return output, normal, inv_std, slope


def backward(grad_output, values, saved, weight_ref, gain, spacing, weight_grad_ref):
    normal, inv_std, slope = saved
    width = values.shape[1]
    scaled = grad_output * slope
    gain_grad = jnp.sum(scaled * normal, axis=0, keepdims=True)
    back = scaled * gain
    before = inv_std * (
        back
        - jnp.mean(back, axis=-1, keepdims=True)
        - normal * jnp.mean(back * normal, axis=-1, keepdims=True)
    )
    grad_input = jnp.zeros(values.shape, F32)
    taken = values.astype(BF16)
    for k, tap in enumerate(rolled(before, -spacing)):
        rows = slice(k * width, (k + 1) * width)
        grad_input += lax.dot_general(
            tap, weight_ref[rows, :], (((1,), (1,)), ((), ())), preferred_element_type=F32
        )
        weight_grad_ref[rows, :] += lax.dot_general(
            taken, tap, (((0,), (0,)), ((), ())), preferred_element_type=F32
        )
    return grad_input, gain_grad


def block_kernel(
    length, place_ref, got_ref, w1_ref, g1_ref, w2_ref, g2_ref, top_ref,
    out_ref, grad_ref, dw1_ref, dw2_ref, gains_ref, wide, total,
):
    items, width = out_ref.shape
    slots = got_ref.shape[0]
    step = slots // 16

    @pl.loop(0, 16)
    def _(c):
        widen(got_ref, wide, step, pl.multiple_of(c * step, 16))

    sessions = items // length

    @pl.loop(0, items // 40)
    def _(g):
        session = g // (length // 40)
        at = session * PITCH + (g - session * (length // 40)) * 40
        to = pl.multiple_of(g * 80, 16)
        for k in range(40):
            a, b, c = [wide[pair(place_ref[t * sessions * PITCH + at + k]), :] for t in range(3)]
            total[pl.ds(to + 2 * k, 2), :] = a + b + c

    dw1_ref[...] = jnp.zeros(dw1_ref.shape, F32)
    dw2_ref[...] = jnp.zeros(dw2_ref.shape, F32)
    gains_ref[...] = jnp.zeros(gains_ref.shape, F32)
    chunk = 2 * length
    pitch = length + PAD
    row = lax.broadcasted_iota(I32, (2 * pitch, width), 0)
    real = ((row >= PAD) & (row < pitch)) | (row >= pitch + PAD)
    g1, g2 = g1_ref[...], g2_ref[...]

    @pl.loop(0, items // chunk)
    def _(c):
        at = pl.ds(pl.multiple_of(c * chunk, 16), chunk)
        embedded = jnp.concatenate(
            [total[pl.ds(2 * c * chunk + h, chunk, stride=2), :] for h in range(2)], axis=1
        )
        embedded = padded(embedded.astype(BF16).astype(F32), length)
        act_one, *saved_one = forward(embedded, w1_ref, g1, 1)
        hidden = jnp.where(real, act_one, 0.0).astype(BF16).astype(F32)
        act_two, *saved_two = forward(hidden, w2_ref, g2, 2)
        out_ref[at, :] = unpadded(embedded + act_two, length).astype(BF16)
        top = padded(top_ref[at, :].astype(F32), length)
        grad_hidden, gain_two = backward(top, hidden, saved_two, w2_ref, g2, 2, dw2_ref)
        grad_hidden = jnp.where(real, grad_hidden, 0.0)
        grad_inner, gain_one = backward(grad_hidden, embedded, saved_one, w1_ref, g1, 1, dw1_ref)
        grad_ref[at, :] = unpadded(top + grad_inner, length).astype(BF16)
        gains_ref[0:1, :] += gain_one
        gains_ref[1:2, :] += gain_two


def block_pass(place, got, length, weight_one, gain_one, weight_two, gain_two, grad_top):
    items, width = grad_top.shape
    operands = (got, weight_one, gain_one.reshape(1, -1), weight_two, gain_two.reshape(1, -1), grad_top)
    shapes = [
        ((items, width), BF16),
        ((items, width), BF16),
        (weight_one.shape, F32),
        (weight_two.shape, F32),
        ((8, width), F32),
    ]
    return pl.pallas_call(
        functools.partial(block_kernel, length),
        out_shape=[jax.ShapeDtypeStruct(*shape) for shape in shapes],
        grid_spec=pltpu.PrefetchScalarGridSpec(
            num_scalar_prefetch=1,
            grid=(1,),
            in_specs=[whole(operand.shape) for operand in operands],
            out_specs=[whole(shape) for shape, _ in shapes],
            scratch_shapes=[pltpu.VMEM((2 * got.shape[0], 128), F32), pltpu.VMEM((2 * items, 128), F32)],
        ),
        cost_estimate=pl.CostEstimate(flops=4 * 10**9, bytes_accessed=30 * 10**6, transcendentals=10**6),
        name="block_pass",
    )(place, *operands)


def collect_kernel(ways, cap, idx_ref, got_ref, out_ref, wide, *accs):
    b = pl.program_id(0)
    block = got_ref.shape[0]
    rows = accs[0].shape[0] // 2 - EDGE

    @pl.when(b == 0)
    def _():
        @pl.loop(0, rows // 256)
        def _(c):
            for acc in accs:
                acc[pl.ds(pl.multiple_of(2 * EDGE + c * 512, 16), 512), :] = jnp.zeros((512, 128), F32)

    widen(got_ref, wide, block)

    @pl.loop(0, block // cap)
    def _(g):
        at = pl.multiple_of(g * (2 * cap), 16)
        base = (b * (block // cap) + g) * PITCH
        for k in range(0, cap, ways):
            spots = [pair(idx_ref[base + k + j]) for j in range(ways)]
            olds = [accs[j][spots[j], :] for j in range(ways)]
            adds = [wide[pl.ds(at + 2 * (k + j), 2), :] for j in range(ways)]
            for j in range(ways):
                accs[j][spots[j], :] = olds[j] + adds[j]

    @pl.when(b == pl.num_programs(0) - 1)
    def _():
        @pl.loop(0, rows // 256)
        def _(c):
            per = out_ref.shape[2] // 256
            to = pl.ds(pl.multiple_of((c % per) * 256, 256), 256)
            for half in range(2):
                at = pl.ds(2 * EDGE + c * 512 + half, 256, stride=2)
                total = accs[0][at, :]
                for acc in accs[1:]:
                    total = total + acc[at, :]
                out_ref[c // per, 128 * half : 128 * half + 128, to] = total.T.astype(BF16)


def collect(idx, got, rows, cap, block=2432, ways=4):
    n, width = got.shape
    shape = (3, width, rows // 3)
    return pl.pallas_call(
        functools.partial(collect_kernel, ways, cap),
        out_shape=jax.ShapeDtypeStruct(shape, BF16),
        grid_spec=pltpu.PrefetchScalarGridSpec(
            num_scalar_prefetch=1,
            grid=(n // block,),
            in_specs=[pl.BlockSpec((block, width), lambda b, i: (b, 0))],
            out_specs=whole(shape),
            scratch_shapes=[pltpu.VMEM((2 * block, 128), F32)]
            + [pltpu.VMEM((2 * (rows + EDGE), 128), F32)] * ways,
        ),
        cost_estimate=pl.CostEstimate(flops=10**7, bytes_accessed=60 * 10**6, transcendentals=0),
        name="collect",
    )(idx, got)


def peer_of(axis, step):
    name, size, stride = AXES[axis]
    index = lax.axis_index(name)
    mine = lax.rem(lax.div(index, stride), size)
    other = lax.rem(mine + step, size)
    return mine, other, {name: index + (other - mine) * stride}


def visit(step):
    (_, ysize, ystride), (_, zsize, zstride), (_, csize, _) = AXES[1:]
    me = lax.axis_index("table")
    y, z, c = lax.div(me, ystride), lax.rem(lax.div(me, zstride), zsize), lax.rem(me, csize)
    turn = lax.rem(step, zsize)
    half = lax.div(turn + 1, 2)
    away = jnp.where(lax.rem(turn, 2) == 1, half, zsize - half)
    y = lax.rem(y + lax.rem(lax.div(step, zsize), ysize), ysize)
    z = lax.rem(z + away, zsize)
    c = lax.rem(c + lax.div(step, zsize * ysize), csize)
    return y * ystride + z * zstride + c


def remote(src, dst, send, recv, device):
    return pltpu.make_async_remote_copy(
        src_ref=src, dst_ref=dst, send_sem=send, recv_sem=recv, device_id=device, device_id_type=MESH
    )


def exchange_kernel(scale, idx_ref, table_ref, *rest):
    summing = scale is not None
    if summing:
        w1_ref, w2_ref, gains_ref, got_ref, out_ref, wide, stage, held, own_sem, sends, recv, *more = rest
        part, r0, s0, r1, s1, r2, a2, a1, *sems = more
    else:
        got_ref, wide, stage, held, own_sem, sends, recv = rest
    shards, cap, width = held.shape
    rows = table_ref.shape[0]
    me = lax.axis_index("table")
    group = GROUP
    total = shards - 1

    barrier = pltpu.get_barrier_semaphore()

    def hello(step, _):
        pl.semaphore_signal(barrier, inc=1, device_id={"table": visit(step)}, device_id_type=MESH)
        return 0

    lax.fori_loop(1, shards, hello, 0)
    if summing:
        for step in range(1, AXES[0][1]):
            pl.semaphore_signal(barrier, inc=1, device_id=peer_of(0, step)[2], device_id_type=MESH)

    def widened(c, _):
        at = pl.ds(pl.multiple_of(c * 64, 64), 64)
        wide[pl.ds(pl.multiple_of(EDGE + c * 64, EDGE), 64), :] = table_ref[at, :].astype(F32)
        return 0

    wide[0:EDGE, :] = jnp.zeros((EDGE, width), F32)

    lax.fori_loop(0, rows // 64, widened, 0)
    if summing:
        parts = [(w1_ref, w1_ref.shape[0]), (w2_ref, w2_ref.shape[0]), (gains_ref, 1)]
        ysize, zcsize = part.shape[1:3]
        block = 0
        for ref, count in parts:
            done = 0
            while done < count:
                many = min(count - done, zcsize - block % zcsize)
                first = block % zcsize
                row = ref[...][None] if ref is gains_ref else ref[done : done + many]
                part[block // (ysize * zcsize), block // zcsize % ysize, first : first + many] = row
                done, block = done + many, block + many
        while block < part.shape[0] * ysize * zcsize:
            many = zcsize - block % zcsize
            empty = jnp.zeros((many,) + part.shape[3:], F32)
            part[block // (ysize * zcsize), block // zcsize % ysize, block % zcsize :] = empty
            block += many
        ymine, zcmine = lax.div(me, zcsize), lax.rem(me, zcsize)
        xmine = peer_of(0, 1)[0]
        xpeers = [peer_of(0, step)[1:] for step in range(1, AXES[0][1])]
        ypeers = [lax.rem(ymine + step, ysize) for step in range(1, ysize)]
        ypeers = [(other, {"table": other * zcsize + zcmine}) for other in ypeers]
        zcpeers = [lax.rem(zcmine + step, zcsize) for step in range(1, zcsize)]
        zcpeers = [(other, {"table": ymine * zcsize + other}) for other in zcpeers]

        def fan(stage, peers, src, dst):
            send_sem, recv_sem = sems[2 * stage : 2 * stage + 2]
            copies = [
                remote(src(other), dst(n), send_sem.at[n], recv_sem.at[n], device)
                for n, (other, device) in enumerate(peers)
            ]
            for copy in copies:
                copy.start()
            return copies

        def landed(copies):
            for copy in copies:
                copy.wait_recv()

    def gather(step):
        dest = visit(step)
        for k in range(0, cap, 8):
            rows8 = [wide[pl.ds(idx_ref[dest * PITCH + k + j], 1), :] for j in range(8)]
            stage[k : k + 8, :] = jnp.concatenate(rows8, axis=0)
        held[step] = stage[...].astype(BF16)

    def post(step):
        remote(
            held.at[step],
            got_ref.at[me],
            sends.at[lax.div(step - 1, group)],
            recv,
            {"table": visit(step)},
        ).start()

    def sent(number, count):
        ref = held.at[pl.ds(0, count)]
        remote(ref, ref, sends.at[number], recv, {"table": visit(1)}).wait_send()

    gather(0)
    own = pltpu.make_async_copy(held.at[0], got_ref.at[me], own_sem)
    gather(1)
    pl.semaphore_wait(barrier, total + (AXES[0][1] - 1 if summing else 0))
    own.start()
    if summing:
        flights = [fan(0, xpeers, lambda other: part.at[other], lambda n: r0.at[n])]

    def go(step, _):
        gather(step)
        post(step - 1)
        return 0

    groups = -(-total // group)
    for number in range(groups):
        if summing and number >= 2:
            sent(number - 2, group)
        low, high = number * group + 2, min((number + 1) * group + 1, shards - 1)
        lax.fori_loop(low, high + 1, go, 0)
        if number == groups - 1:
            post(shards - 1)
        if summing and number >= 1:
            for stage in range(number, number + 1) if number < groups - 1 else range(number, 6):
                if stage > 5:
                    continue
                landed(flights[-1])
                if stage == 1:
                    s0[...] = sum([r0[n] for n in range(len(xpeers))], part[xmine])
                    flights.append(fan(1, ypeers, lambda other: s0.at[other], lambda n: r1.at[n]))
                elif stage == 2:
                    s1[...] = sum([r1[n] for n in range(len(ypeers))], s0[ymine])
                    flights.append(fan(2, zcpeers, lambda other: s1.at[other], lambda n: r2.at[n]))
                elif stage == 3:
                    a2[zcmine] = sum([r2[n] for n in range(len(zcpeers))], s1[zcmine]) * scale
                    flights.append(fan(3, zcpeers, lambda _: a2.at[zcmine], lambda _: a2.at[zcmine]))
                elif stage == 4:
                    flights.append(fan(4, ypeers, lambda _: a2, lambda _: a1.at[ymine]))
                    a1[ymine] = a2[...]
                elif stage == 5:
                    flights.append(fan(5, xpeers, lambda _: a1, lambda _: out_ref.at[xmine]))
                    out_ref[xmine] = a1[...]
    for number in range(groups):
        if not summing or number >= groups - 2:
            sent(number, min(group, total - number * group))
    own.wait()
    ref = held.at[pl.ds(0, total)]
    remote(ref, got_ref.at[pl.ds(0, total)], sends.at[0], recv, {"table": visit(1)}).wait_recv()
    if summing:
        landed(flights[-1])
        for copies in flights:
            for copy in copies:
                copy.wait_send()


def exchange(idx, table, shards, cap, collective_id, name, sums=None):
    rows, width = table.shape
    any_space, vmem = pl.BlockSpec(memory_space=pl.ANY), pl.BlockSpec(memory_space=pltpu.VMEM)
    out_shape = [jax.ShapeDtypeStruct((shards, cap, width), BF16)]
    out_specs = [any_space]
    scratch = [
        pltpu.VMEM((rows + EDGE, width), F32),
        pltpu.VMEM((cap, width), F32),
        pltpu.VMEM((shards, cap, width), BF16),
        pltpu.SemaphoreType.DMA,
        pltpu.SemaphoreType.DMA((-(-(shards - 1) // GROUP),)),
        pltpu.SemaphoreType.DMA,
    ]
    operands, scale = [], None
    if sums is not None:
        *operands, scale = sums
        xsize, ysize, zcsize = AXES[0][1], AXES[1][1], AXES[1][2]
        tile = operands[0].shape[1:]
        line, plane = (zcsize,) + tile, (ysize, zcsize) + tile
        out_shape.append(jax.ShapeDtypeStruct((xsize,) + plane, F32))
        out_specs.append(vmem)
        shapes = [(xsize,) + plane, (xsize - 1,) + plane, plane, (ysize - 1,) + line, line]
        shapes += [(zcsize - 1,) + tile, line, plane]
        scratch += [pltpu.VMEM(shape, F32) for shape in shapes]
        for size in (xsize, ysize, zcsize, zcsize, ysize, xsize):
            scratch += [pltpu.SemaphoreType.DMA((size - 1,))] * 2
    return pl.pallas_call(
        functools.partial(exchange_kernel, scale),
        out_shape=out_shape,
        in_specs=[pl.BlockSpec(memory_space=pltpu.SMEM)] + [vmem] * (1 + len(operands)),
        out_specs=out_specs,
        scratch_shapes=scratch,
        compiler_params=pltpu.CompilerParams(collective_id=collective_id, has_side_effects=True),
        cost_estimate=pl.CostEstimate(flops=10**7, bytes_accessed=10**8, transcendentals=0),
        name=name,
    )(idx, table, *operands)


def greet(steps):
    barrier = pltpu.get_barrier_semaphore()
    for axis, step in steps:
        pl.semaphore_signal(barrier, inc=1, device_id=peer_of(axis, step)[2], device_id_type=MESH)
    pl.semaphore_wait(barrier, len(steps))


def group_sum_kernel(dense_ref, out_ref, far, mixed, near, sems):
    tables, quarter, _ = out_ref.shape
    half = quarter // 2
    greet([(0, step) for step in range(1, 4)])
    mine, after, right = peer_of(0, 1)
    _, across, _ = peer_of(0, 2)
    _, before, left = peer_of(0, 3)
    ways = ((right, after, 0), (left, before, half))

    def share(t, owner, start):
        return dense_ref.at[t, pl.ds(pl.multiple_of(owner * quarter + start, half), half)]

    def hop(kind, t, way, src, dst):
        n = (kind * tables + t) * 2 + way
        copy = remote(src, dst, sems.at[0, n], sems.at[1, n], ways[way][0])
        copy.start()
        return copy

    firsts = [
        [hop(0, t, way, share(t, across, start), far.at[t, way]) for way, (_, _, start) in enumerate(ways)]
        for t in range(tables)
    ]
    others = [
        [
            hop(1, t, way, share(t, owner, half - start), near.at[t, way, pl.ds(half - start, half)])
            for way, (_, owner, start) in enumerate(ways)
        ]
        for t in range(tables)
    ]
    lasts = []
    for t in range(tables):
        for way, (_, owner, start) in enumerate(ways):
            firsts[t][way].wait_recv()
            kept = dense_ref[t, pl.ds(pl.multiple_of(owner * quarter + start, half), half), :]
            mixed[t, way] = (far[t, way].astype(F32) + kept.astype(F32)).astype(BF16)
        lasts.append(
            [hop(2, t, way, mixed.at[t, way], near.at[t, way, pl.ds(start, half)]) for way, (_, _, start) in enumerate(ways)]
        )
    for t in range(tables):
        for way in range(2):
            others[t][way].wait_recv()
            lasts[t][way].wait_recv()
        kept = dense_ref[t, pl.ds(pl.multiple_of(mine * quarter, quarter), quarter), :]
        out_ref[t] = kept.astype(F32) + near[t, 0].astype(F32) + near[t, 1].astype(F32)
    for copies in firsts + others + lasts:
        for copy in copies:
            copy.wait_send()


def group_sum(dense):
    tables, width, rows = dense.shape
    quarter = width // 4
    return pl.pallas_call(
        group_sum_kernel,
        out_shape=jax.ShapeDtypeStruct((tables, quarter, rows), F32),
        in_specs=[pl.BlockSpec(memory_space=pltpu.VMEM)],
        out_specs=pl.BlockSpec(memory_space=pltpu.VMEM),
        scratch_shapes=[
            pltpu.VMEM((tables, 2, quarter // 2, rows), BF16),
            pltpu.VMEM((tables, 2, quarter // 2, rows), BF16),
            pltpu.VMEM((tables, 2, quarter, rows), BF16),
            pltpu.SemaphoreType.DMA((2, 6 * tables)),
        ],
        compiler_params=pltpu.CompilerParams(collective_id=2, has_side_effects=True),
        cost_estimate=pl.CostEstimate(flops=10**6, bytes_accessed=60 * 10**6, transcendentals=0),
        name="group_sum",
    )(dense)


def on_device(shard_of, offsets, table, weight_one, gain_one, weight_two, gain_two, grad_out):
    sessions, length, _ = shard_of.shape
    width = table.shape[2]
    rows_dev = table.shape[1]
    rows = 3 * rows_dev
    item_count = sessions * length
    shards = lax.axis_size("table")
    groups = lax.axis_size("dp")
    slot_count = 8 * ((6 * item_count + 8 * shards - 1) // (8 * shards))
    place, asked, items = make_index(
        jnp.transpose(shard_of, (2, 0, 1)), jnp.transpose(offsets, (2, 0, 1)), shards, slot_count, rows_dev
    )
    asked = asked.reshape(-1)
    (got,) = exchange(asked, table.reshape(rows, width), shards, slot_count, 0, "rows_out")
    scale = 1.0 / math.sqrt(item_count * groups * shards)
    block_out, grad_embed, first_weights, second_weights, gains = block_pass(
        place.reshape(-1),
        got.reshape(-1, width),
        length,
        weight_one,
        gain_one,
        weight_two,
        gain_two,
        grad_out.reshape(item_count, width),
    )
    tiles = (-1, 8, width)
    arrived, totals = exchange(
        items.reshape(-1),
        grad_embed,
        shards,
        slot_count,
        1,
        "grads_out",
        (first_weights.reshape(tiles), second_weights.reshape(tiles), gains, scale),
    )
    totals = totals.reshape(-1, width)
    dense = collect(asked, arrived.reshape(-1, width), rows, slot_count)
    table_grad = jnp.transpose(group_sum(dense), (0, 2, 1))
    block_out = block_out.reshape(sessions, length, width)
    return block_out, totals[:768], totals[768:1536], totals[1536], totals[1537], table_grad


def solution(mesh):
    placed = (
        P(("dp", "table"), None, None),
        P(("dp", "table"), None, None),
        P(None, "table", None),
        P(),
        P(),
        P(),
        P(),
        P(("dp", "table"), None, None),
    )
    return jax.shard_map(
        on_device,
        mesh=mesh,
        in_specs=placed,
        out_specs=(P(("dp", "table"), None, None), P(), P(), P(), P(), P(None, "table", "dp")),
        check_vma=False,
    )
```

```python
import functools
import math

import jax
import jax.numpy as jnp
from jax import lax
from jax.experimental import pallas as pl
from jax.experimental.pallas import tpu as pltpu
from jax.sharding import PartitionSpec as P

F32, BF16, I32 = jnp.float32, jnp.bfloat16, jnp.int32
MESH = pl.DeviceIdType.MESH
GELU_C = 0.7978845608028654
GELU_K = 0.044715
PITCH = 256
EDGE = 8
AXES = (("dp", 4, 1), ("table", 4, 16), ("table", 8, 2), ("table", 2, 1))


def gelu_parts(inputs):
    inner = GELU_C * (inputs + GELU_K * inputs * inputs * inputs)
    tangent = jnp.tanh(inner)
    output = 0.5 * inputs * (1.0 + tangent)
    slope = 0.5 * (1.0 + tangent) + 0.5 * inputs * (1.0 - tangent * tangent) * GELU_C * (
        1.0 + 3.0 * GELU_K * inputs * inputs
    )
    return (output, slope)


def index_kernel(cap, rows_dev, sh_ref, off_ref, place_ref, asked_ref, lists_ref, req_ref, item_ref, send, recv, list_send, list_recv):
    tables, sessions, length = sh_ref.shape
    shards = asked_ref.shape[0]
    me = lax.axis_index("table")
    barrier = pltpu.get_barrier_semaphore()

    def hello(step, _):
        pl.semaphore_signal(barrier, inc=1, device_id={"table": visit(step)}, device_id_type=MESH)
        return 0

    lax.fori_loop(1, shards, hello, 0)
    tri = (
        lax.broadcasted_iota(I32, (length, length), 0) < lax.broadcasted_iota(I32, (length, length), 1)
    ).astype(BF16)
    lane = lax.broadcasted_iota(I32, (1, length), 1)
    shard_id = lax.broadcasted_iota(I32, (shards, length), 0)
    slot_id = lax.broadcasted_iota(I32, (cap, length), 0)
    base = jnp.zeros((shards, 1), F32)
    listed = [jnp.zeros((shards, cap), F32) for _ in range(4)]
    dims = (((1,), (1,)), ((), ()))
    for t in range(tables):
        for s in range(sessions):
            sh = sh_ref[t, s : s + 1, :]
            code = off_ref[t, s : s + 1, :] + (t * rows_dev + EDGE)
            item = lane + (s * length + EDGE)
            hit = shard_id == sh
            hot = jnp.where(hit, 1.0, 0.0)
            hot16 = hot.astype(BF16)
            prefix = jnp.dot(hot16, tri, preferred_element_type=F32) + base
            rank = jnp.sum(jnp.where(hit, prefix, 0.0), axis=0, keepdims=True).astype(I32)
            base = base + jnp.sum(hot, axis=1, keepdims=True)
            place = sh * cap + rank
            place_ref[t * sessions + s, 0:1, :] = place[:, :128]
            place_ref[t * sessions + s, 1:2, 0 : length - 128] = place[:, 128:]
            here = slot_id == rank
            for n, digit in enumerate((code // 256, code % 256, item // 256, item % 256)):
                listed[n] += lax.dot_general(
                    hot16,
                    jnp.where(here, digit.astype(F32), 0.0).astype(BF16),
                    dims,
                    preferred_element_type=F32,
                )
    for ref, high, low in ((req_ref, listed[0], listed[1]), (item_ref, listed[2], listed[3])):
        codes = (high * 256.0 + low).astype(I32)
        ref[...] = jnp.zeros(ref.shape, I32)
        ref[:, 0, :] = codes[:, :128]
        ref[:, 1, 0 : cap - 128] = codes[:, 128:]
    pl.semaphore_wait(barrier, shards - 1)

    def ask(step, _):
        dest = visit(step)
        remote(req_ref.at[dest], asked_ref.at[me], send, recv, {"table": dest}).start()
        return 0

    lax.fori_loop(1, shards, ask, 0)
    asked_ref[me] = req_ref[me]
    ymine, zmine, cmine = spot()
    zsize, plane = lists_ref.shape[:2]

    def tell(step, _):
        z = lax.rem(zmine + step, zsize)
        for k in range(plane):
            source = item_ref.at[device_at(*plane_spot(k), z)]
            remote(source, lists_ref.at[zmine, k], list_send, list_recv, {"table": device_at(ymine, cmine, z)}).start()
        return 0

    lax.fori_loop(1, zsize, tell, 0)
    for k in range(plane):
        lists_ref[zmine, k] = item_ref[device_at(*plane_spot(k), zmine)]
    many = pl.ds(0, shards - 1)
    remote(req_ref.at[many], asked_ref.at[many], send, recv, {"table": visit(1)}).wait()
    many = item_ref.at[pl.ds(0, shards - plane)]
    remote(many, many, list_send, list_recv, {"table": visit(1)}).wait()


def make_index(sh, off, shards, cap, rows_dev):
    tables, sessions, _ = sh.shape
    block = jax.ShapeDtypeStruct((shards, 2, 128), I32)
    zsize = AXES[2][1]
    lists = jax.ShapeDtypeStruct((zsize, shards // zsize, 2, 128), I32)
    vmem = pl.BlockSpec(memory_space=pltpu.VMEM)
    return pl.pallas_call(
        functools.partial(index_kernel, cap, rows_dev),
        out_shape=(jax.ShapeDtypeStruct((tables * sessions, 2, 128), I32), block, lists),
        in_specs=[vmem] * 2,
        out_specs=[vmem] * 3,
        scratch_shapes=[pltpu.VMEM((shards, 2, 128), I32)] * 2 + [pltpu.SemaphoreType.DMA] * 4,
        compiler_params=pltpu.CompilerParams(collective_id=3, has_side_effects=True),
        cost_estimate=pl.CostEstimate(flops=10**9, bytes_accessed=10**6, transcendentals=0),
        name="index",
    )(sh, off)


def whole(shape):
    zeros = (0,) * len(shape)
    return pl.BlockSpec(shape, lambda b, i: zeros, pipeline_mode=pl.Buffered(1))


def widen(src, dst, rows, at=0):
    values = src[pl.ds(at, rows), :].astype(F32)
    dst[pl.ds(2 * at, rows, stride=2), :] = values[:, :128]
    dst[pl.ds(2 * at + 1, rows, stride=2), :] = values[:, 128:]


def pair(index):
    return pl.ds(pl.multiple_of(2 * index, 2), 2)


PAD = 8


def padded(values, length):
    zeros = jnp.zeros((PAD, values.shape[1]), F32)
    parts = []
    for start in range(0, values.shape[0], length):
        parts += [zeros, values[start : start + length]]
    return jnp.concatenate(parts, axis=0)


def unpadded(values, length):
    pitch = length + PAD
    return jnp.concatenate(
        [values[start + PAD : start + pitch] for start in range(0, values.shape[0], pitch)], axis=0
    )


def rolled(values, by):
    return [values.astype(BF16)] + [
        pltpu.roll(values, (k * by) % values.shape[0], 0).astype(BF16) for k in (1, 2)
    ]


def normalized(before):
    centred = before - jnp.mean(before, axis=-1, keepdims=True)
    inv_std = lax.rsqrt(jnp.mean(centred * centred, axis=-1, keepdims=True) + 1e-05)
    return centred * inv_std, inv_std


def forward(values, weight_ref, gain, spacing):
    width = values.shape[1]
    before = jnp.zeros(values.shape, F32)
    for k, tap in enumerate(rolled(values, spacing)):
        before += jnp.dot(tap, weight_ref[k * width : (k + 1) * width, :], preferred_element_type=F32)
    normal, inv_std = normalized(before)
    output, slope = gelu_parts(normal * gain)
    return output, normal, inv_std, slope


def backward(grad_output, values, saved, weight_ref, gain, spacing, weight_grad_ref):
    normal, inv_std, slope = saved
    width = values.shape[1]
    scaled = grad_output * slope
    gain_grad = jnp.sum(scaled * normal, axis=0, keepdims=True)
    back = scaled * gain
    before = inv_std * (
        back
        - jnp.mean(back, axis=-1, keepdims=True)
        - normal * jnp.mean(back * normal, axis=-1, keepdims=True)
    )
    grad_input = jnp.zeros(values.shape, F32)
    taken = values.astype(BF16)
    for k, tap in enumerate(rolled(before, -spacing)):
        rows = slice(k * width, (k + 1) * width)
        grad_input += lax.dot_general(
            tap, weight_ref[rows, :], (((1,), (1,)), ((), ())), preferred_element_type=F32
        )
        weight_grad_ref[rows, :] += lax.dot_general(
            taken, tap, (((0,), (0,)), ((), ())), preferred_element_type=F32
        )
    return grad_input, gain_grad


def block_kernel(
    length, place_ref, got_ref, w1_ref, g1_ref, w2_ref, g2_ref, top_ref,
    out_ref, grad_ref, dw1_ref, dw2_ref, gains_ref, wide, total,
):
    items, width = out_ref.shape
    slots = got_ref.shape[0]
    step = slots // 16

    @pl.loop(0, 16)
    def _(c):
        widen(got_ref, wide, step, pl.multiple_of(c * step, 16))

    sessions = items // length

    @pl.loop(0, items // 40)
    def _(g):
        session = g // (length // 40)
        at = session * PITCH + (g - session * (length // 40)) * 40
        to = pl.multiple_of(g * 80, 16)
        for k in range(40):
            a, b, c = [wide[pair(place_ref[t * sessions * PITCH + at + k]), :] for t in range(3)]
            total[pl.ds(to + 2 * k, 2), :] = a + b + c

    dw1_ref[...] = jnp.zeros(dw1_ref.shape, F32)
    dw2_ref[...] = jnp.zeros(dw2_ref.shape, F32)
    gains_ref[...] = jnp.zeros(gains_ref.shape, F32)
    chunk = 2 * length
    pitch = length + PAD
    row = lax.broadcasted_iota(I32, (2 * pitch, width), 0)
    real = ((row >= PAD) & (row < pitch)) | (row >= pitch + PAD)
    g1, g2 = g1_ref[...], g2_ref[...]

    @pl.loop(0, items // chunk)
    def _(c):
        at = pl.ds(pl.multiple_of(c * chunk, 16), chunk)
        embedded = jnp.concatenate(
            [total[pl.ds(2 * c * chunk + h, chunk, stride=2), :] for h in range(2)], axis=1
        )
        embedded = padded(embedded.astype(BF16).astype(F32), length)
        act_one, *saved_one = forward(embedded, w1_ref, g1, 1)
        hidden = jnp.where(real, act_one, 0.0).astype(BF16).astype(F32)
        act_two, *saved_two = forward(hidden, w2_ref, g2, 2)
        out_ref[at, :] = unpadded(embedded + act_two, length).astype(BF16)
        top = padded(top_ref[at, :].astype(F32), length)
        grad_hidden, gain_two = backward(top, hidden, saved_two, w2_ref, g2, 2, dw2_ref)
        grad_hidden = jnp.where(real, grad_hidden, 0.0)
        grad_inner, gain_one = backward(grad_hidden, embedded, saved_one, w1_ref, g1, 1, dw1_ref)
        grad_ref[at, :] = unpadded(top + grad_inner, length).astype(BF16)
        gains_ref[0:1, :] += gain_one
        gains_ref[1:2, :] += gain_two


def block_pass(place, got, length, weight_one, gain_one, weight_two, gain_two, grad_top):
    items, width = grad_top.shape
    operands = (got, weight_one, gain_one.reshape(1, -1), weight_two, gain_two.reshape(1, -1), grad_top)
    shapes = [
        ((items, width), BF16),
        ((items, width), BF16),
        (weight_one.shape, F32),
        (weight_two.shape, F32),
        ((8, width), F32),
    ]
    return pl.pallas_call(
        functools.partial(block_kernel, length),
        out_shape=[jax.ShapeDtypeStruct(*shape) for shape in shapes],
        grid_spec=pltpu.PrefetchScalarGridSpec(
            num_scalar_prefetch=1,
            grid=(1,),
            in_specs=[whole(operand.shape) for operand in operands],
            out_specs=[whole(shape) for shape, _ in shapes],
            scratch_shapes=[pltpu.VMEM((2 * got.shape[0], 128), F32), pltpu.VMEM((2 * items, 128), F32)],
        ),
        cost_estimate=pl.CostEstimate(flops=4 * 10**9, bytes_accessed=30 * 10**6, transcendentals=10**6),
        name="block_pass",
    )(place, *operands)


def collect_kernel(ways, cap, idx_ref, got_ref, out_ref, wide, *accs):
    b = pl.program_id(0)
    block = got_ref.shape[0]
    rows = accs[0].shape[0] // 2 - EDGE

    @pl.when(b == 0)
    def _():
        @pl.loop(0, rows // 256)
        def _(c):
            for acc in accs:
                acc[pl.ds(pl.multiple_of(2 * EDGE + c * 512, 16), 512), :] = jnp.zeros((512, 128), F32)

    widen(got_ref, wide, block)

    @pl.loop(0, block // cap)
    def _(g):
        at = pl.multiple_of(g * (2 * cap), 16)
        base = (b * (block // cap) + g) * PITCH
        for k in range(0, cap, ways):
            spots = [pair(idx_ref[base + k + j]) for j in range(ways)]
            olds = [accs[j][spots[j], :] for j in range(ways)]
            adds = [wide[pl.ds(at + 2 * (k + j), 2), :] for j in range(ways)]
            for j in range(ways):
                accs[j][spots[j], :] = olds[j] + adds[j]

    @pl.when(b == pl.num_programs(0) - 1)
    def _():
        @pl.loop(0, rows // 256)
        def _(c):
            per = out_ref.shape[2] // 256
            to = pl.ds(pl.multiple_of((c % per) * 256, 256), 256)
            for half in range(2):
                at = pl.ds(2 * EDGE + c * 512 + half, 256, stride=2)
                total = accs[0][at, :]
                for acc in accs[1:]:
                    total = total + acc[at, :]
                out_ref[c // per, 128 * half : 128 * half + 128, to] = total.T.astype(BF16)


def collect(idx, got, rows, cap, block=2432, ways=4):
    n, width = got.shape
    shape = (3, width, rows // 3)
    return pl.pallas_call(
        functools.partial(collect_kernel, ways, cap),
        out_shape=jax.ShapeDtypeStruct(shape, BF16),
        grid_spec=pltpu.PrefetchScalarGridSpec(
            num_scalar_prefetch=1,
            grid=(n // block,),
            in_specs=[pl.BlockSpec((block, width), lambda b, i: (b, 0))],
            out_specs=whole(shape),
            scratch_shapes=[pltpu.VMEM((2 * block, 128), F32)]
            + [pltpu.VMEM((2 * (rows + EDGE), 128), F32)] * ways,
        ),
        cost_estimate=pl.CostEstimate(flops=10**7, bytes_accessed=60 * 10**6, transcendentals=0),
        name="collect",
    )(idx, got)


def peer_of(axis, step):
    name, size, stride = AXES[axis]
    index = lax.axis_index(name)
    mine = lax.rem(lax.div(index, stride), size)
    other = lax.rem(mine + step, size)
    return mine, other, {name: index + (other - mine) * stride}


def visit(step):
    (_, ysize, ystride), (_, zsize, zstride), (_, csize, _) = AXES[1:]
    me = lax.axis_index("table")
    y, z, c = lax.div(me, ystride), lax.rem(lax.div(me, zstride), zsize), lax.rem(me, csize)
    turn = lax.rem(step, zsize)
    half = lax.div(turn + 1, 2)
    away = jnp.where(lax.rem(turn, 2) == 1, half, zsize - half)
    y = lax.rem(y + lax.rem(lax.div(step, zsize), ysize), ysize)
    z = lax.rem(z + away, zsize)
    c = lax.rem(c + lax.div(step, zsize * ysize), csize)
    return y * ystride + z * zstride + c


def spot():
    me = lax.axis_index("table")
    (_, _, ystride), (_, zsize, zstride), (_, csize, _) = AXES[1:]
    return lax.div(me, ystride), lax.rem(lax.div(me, zstride), zsize), lax.rem(me, csize)


def device_at(y, c, z):
    return y * AXES[1][2] + z * AXES[2][2] + c


def plane_spot(k):
    return k // AXES[3][1], k % AXES[3][1]


def remote(src, dst, send, recv, device):
    return pltpu.make_async_remote_copy(
        src_ref=src, dst_ref=dst, send_sem=send, recv_sem=recv, device_id=device, device_id_type=MESH
    )


def exchange_kernel(idx_ref, table_ref, got_ref, wide, stage, held, own_sem, send, recv):
    shards, cap, width = held.shape
    rows = table_ref.shape[0]
    me = lax.axis_index("table")
    total = shards - 1
    barrier = pltpu.get_barrier_semaphore()

    def hello(step, _):
        pl.semaphore_signal(barrier, inc=1, device_id={"table": visit(step)}, device_id_type=MESH)
        return 0

    lax.fori_loop(1, shards, hello, 0)

    def widened(c, _):
        at = pl.ds(pl.multiple_of(c * 64, 64), 64)
        wide[pl.ds(pl.multiple_of(EDGE + c * 64, EDGE), 64), :] = table_ref[at, :].astype(F32)
        return 0

    wide[0:EDGE, :] = jnp.zeros((EDGE, width), F32)
    lax.fori_loop(0, rows // 64, widened, 0)

    def gather(step):
        dest = visit(step)
        for k in range(0, cap, 8):
            rows8 = [wide[pl.ds(idx_ref[dest * PITCH + k + j], 1), :] for j in range(8)]
            stage[k : k + 8, :] = jnp.concatenate(rows8, axis=0)
        held[step] = stage[...].astype(BF16)

    def post(step):
        remote(held.at[step], got_ref.at[me], send, recv, {"table": visit(step)}).start()

    gather(1)
    pl.semaphore_wait(barrier, total)

    def go(step, _):
        gather(step)
        post(step - 1)
        return 0

    lax.fori_loop(2, shards, go, 0)
    post(total)
    gather(0)
    own = pltpu.make_async_copy(held.at[0], got_ref.at[me], own_sem)
    own.start()
    own.wait()
    many = pl.ds(0, total)
    remote(held.at[many], got_ref.at[many], send, recv, {"table": visit(1)}).wait()


def exchange(idx, table, shards, cap, collective_id, name):
    rows, width = table.shape
    return pl.pallas_call(
        exchange_kernel,
        out_shape=jax.ShapeDtypeStruct((shards, cap, width), BF16),
        in_specs=[pl.BlockSpec(memory_space=pltpu.SMEM), pl.BlockSpec(memory_space=pltpu.VMEM)],
        out_specs=pl.BlockSpec(memory_space=pl.ANY),
        scratch_shapes=[
            pltpu.VMEM((rows + EDGE, width), F32),
            pltpu.VMEM((cap, width), F32),
            pltpu.VMEM((shards, cap, width), BF16),
            pltpu.SemaphoreType.DMA,
            pltpu.SemaphoreType.DMA,
            pltpu.SemaphoreType.DMA,
        ],
        compiler_params=pltpu.CompilerParams(collective_id=collective_id, has_side_effects=True),
        cost_estimate=pl.CostEstimate(flops=10**7, bytes_accessed=10**8, transcendentals=0),
        name=name,
    )(idx, table)


def relay_kernel(
    scale, idx_ref, table_ref, w1_ref, w2_ref, gains_ref, got_ref, out_ref,
    blocks, wide, stage, held, own_sem, ring_send, ring_recv, send, recv,
    part, r0, s0, r1, s1, r2, a2, a1, *sems,
):
    zsize, rows, width = blocks.shape
    shards, cap, _ = held.shape
    plane = shards // zsize
    me = lax.axis_index("table")
    ymine, zmine, cmine = spot()
    parts = [(w1_ref, w1_ref.shape[0]), (w2_ref, w2_ref.shape[0]), (gains_ref, 1)]
    ysize, zcsize = part.shape[1:3]
    block = 0
    for ref, count in parts:
        done = 0
        while done < count:
            many = min(count - done, zcsize - block % zcsize)
            first = block % zcsize
            row = ref[...][None] if ref is gains_ref else ref[done : done + many]
            part[block // (ysize * zcsize), block // zcsize % ysize, first : first + many] = row
            done, block = done + many, block + many
    while block < part.shape[0] * ysize * zcsize:
        many = zcsize - block % zcsize
        empty = jnp.zeros((many,) + part.shape[3:], F32)
        part[block // (ysize * zcsize), block // zcsize % ysize, block % zcsize :] = empty
        block += many
    zcmine = lax.rem(me, zcsize)
    xmine = peer_of(0, 1)[0]
    xpeers = [peer_of(0, step)[1:] for step in range(1, AXES[0][1])]
    ypeers = [lax.rem(ymine + step, ysize) for step in range(1, ysize)]
    ypeers = [(other, {"table": other * zcsize + zcmine}) for other in ypeers]
    zcpeers = [lax.rem(zcmine + step, zcsize) for step in range(1, zcsize)]
    zcpeers = [(other, {"table": ymine * zcsize + other}) for other in zcpeers]

    def fan(stage, peers, src, dst):
        send_sem, recv_sem = sems[2 * stage : 2 * stage + 2]
        copies = [
            remote(src(other), dst(n), send_sem.at[n], recv_sem.at[n], device)
            for n, (other, device) in enumerate(peers)
        ]
        for copy in copies:
            copy.start()
        return copies

    def landed(copies):
        for copy in copies:
            copy.wait_recv()

    barrier = pltpu.get_barrier_semaphore()
    others = []
    for dy in range(1, ysize):
        for dc in range(AXES[3][1]):
            y, c = lax.rem(ymine + dy, ysize), lax.rem(cmine + dc, AXES[3][1])
            others.append({"table": device_at(y, c, zmine)})
    known = [device for _, device in xpeers + zcpeers] + others
    for device in known:
        pl.semaphore_signal(barrier, inc=1, device_id=device, device_id_type=MESH)
    wide[0:EDGE, :] = jnp.zeros((EDGE, width), F32)
    pl.semaphore_wait(barrier, len(known))
    right = {"table": device_at(ymine, cmine, lax.rem(zmine + 1, zsize))}
    left = {"table": device_at(ymine, cmine, lax.rem(zmine + zsize - 1, zsize))}
    far = zsize // 2
    half = rows // 2

    def ring(way, hop):
        source = lax.rem(zmine + (zsize - hop if way == 0 else hop), zsize)
        src, dst = table_ref if hop == 0 else blocks.at[source], blocks.at[source]
        if hop == far - 1:
            at = pl.ds(way * half, half)
            src, dst = src.at[at], dst.at[at]
        return remote(src, dst, ring_send.at[way, hop], ring_recv.at[way, hop], right if way == 0 else left)

    copies = {(way, hop): ring(way, hop) for way in range(2) for hop in range(far)}
    flights = [fan(0, xpeers, lambda other: part.at[other], lambda n: r0.at[n])]
    for way in range(2):
        copies[way, 0].start()

    def serve(number, source, rows_ref):
        def widened(c, _):
            at = pl.ds(pl.multiple_of(c * 64, 64), 64)
            wide[pl.ds(pl.multiple_of(EDGE + c * 64, EDGE), 64), :] = rows_ref[at, :].astype(F32)
            return 0

        lax.fori_loop(0, rows // 64, widened, 0)
        origin = device_at(ymine, cmine, source)

        def turned(step):
            y, c = plane_spot(step)
            return lax.rem(ymine + y, ysize), lax.rem(cmine + c, AXES[3][1])

        def gather(step):
            y, c = turned(step)
            base = (source * plane + y * AXES[3][1] + c) * PITCH
            for k in range(0, cap, 8):
                rows8 = [wide[pl.ds(idx_ref[base + k + j], 1), :] for j in range(8)]
                stage[k : k + 8, :] = jnp.concatenate(rows8, axis=0)
            held[number * plane + step] = stage[...].astype(BF16)

        def post(step):
            y, c = turned(step)
            remote(
                held.at[number * plane + step], got_ref.at[origin], send, recv, {"table": device_at(y, c, zmine)}
            ).start()

        def go(step, _):
            gather(step)
            post(step - 1)
            return 0

        gather(1)
        lax.fori_loop(2, plane, go, 0)
        post(plane - 1)
        gather(0)
        own = pltpu.make_async_copy(held.at[number * plane], got_ref.at[origin], own_sem.at[number])
        own.start()
        return own

    def sum_stage(stage_number):
        landed(flights[-1])
        if stage_number == 1:
            s0[...] = sum([r0[n] for n in range(len(xpeers))], part[xmine])
            flights.append(fan(1, ypeers, lambda other: s0.at[other], lambda n: r1.at[n]))
        elif stage_number == 2:
            s1[...] = sum([r1[n] for n in range(len(ypeers))], s0[ymine])
            flights.append(fan(2, zcpeers, lambda other: s1.at[other], lambda n: r2.at[n]))
        elif stage_number == 3:
            a2[zcmine] = sum([r2[n] for n in range(len(zcpeers))], s1[zcmine]) * scale
            flights.append(fan(3, zcpeers, lambda _: a2.at[zcmine], lambda _: a2.at[zcmine]))
        elif stage_number == 4:
            flights.append(fan(4, ypeers, lambda _: a2, lambda _: a1.at[ymine]))
            a1[ymine] = a2[...]
        elif stage_number == 5:
            flights.append(fan(5, xpeers, lambda _: a1, lambda _: out_ref.at[xmine]))
            out_ref[xmine] = a1[...]

    locals_ = [serve(0, zmine, table_ref)]
    number, done = 1, 0
    for hop in range(1, far + 1):
        if hop < far:
            for way in range(2):
                copies[way, hop - 1].wait_recv()
                copies[way, hop].start()
                source = lax.rem(zmine + (zsize - hop if way == 0 else hop), zsize)
                locals_.append(serve(number, source, blocks.at[source]))
                number += 1
                if done < 5:
                    done += 1
                    sum_stage(done)
        else:
            while done < 5:
                done += 1
                sum_stage(done)
            source = lax.rem(zmine + far, zsize)
            for way in range(2):
                copies[way, hop - 1].wait_recv()
            locals_.append(serve(number, source, blocks.at[source]))
    for copy in copies.values():
        copy.wait_send()
    for copy in locals_:
        copy.wait()
    many = pl.ds(0, shards - zsize)
    remote(held.at[many], got_ref.at[many], send, recv, right).wait()
    landed(flights[-1])
    for flight in flights:
        for copy in flight:
            copy.wait_send()


def relay(idx, table, shards, cap, w1, w2, gains, scale):
    rows, width = table.shape
    (xsize, ysize, zsize), zcsize = [AXES[n][1] for n in range(3)], AXES[1][2]
    tile = w1.shape[1:]
    line, plane = (zcsize,) + tile, (ysize, zcsize) + tile
    shapes = [(xsize,) + plane, (xsize - 1,) + plane, plane, (ysize - 1,) + line, line]
    shapes += [(zcsize - 1,) + tile, line, plane]
    dma = pltpu.SemaphoreType.DMA
    scratch = [
        pltpu.VMEM((zsize, rows, width), BF16),
        pltpu.VMEM((rows + EDGE, width), F32),
        pltpu.VMEM((cap, width), F32),
        pltpu.VMEM((shards, cap, width), BF16),
        dma((zsize,)),
        dma((2, zsize // 2)),
        dma((2, zsize // 2)),
        dma,
        dma,
    ]
    scratch += [pltpu.VMEM(shape, F32) for shape in shapes]
    for size in (xsize, ysize, zcsize, zcsize, ysize, xsize):
        scratch += [dma((size - 1,))] * 2
    vmem = pl.BlockSpec(memory_space=pltpu.VMEM)
    return pl.pallas_call(
        functools.partial(relay_kernel, scale),
        out_shape=[
            jax.ShapeDtypeStruct((shards, cap, width), BF16),
            jax.ShapeDtypeStruct((xsize,) + plane, F32),
        ],
        in_specs=[pl.BlockSpec(memory_space=pltpu.SMEM)] + [vmem] * 4,
        out_specs=[pl.BlockSpec(memory_space=pl.ANY), vmem],
        scratch_shapes=scratch,
        compiler_params=pltpu.CompilerParams(collective_id=1, has_side_effects=True),
        cost_estimate=pl.CostEstimate(flops=10**7, bytes_accessed=10**8, transcendentals=0),
        name="grads_out",
    )(idx, table, w1, w2, gains)


def greet(steps):
    barrier = pltpu.get_barrier_semaphore()
    for axis, step in steps:
        pl.semaphore_signal(barrier, inc=1, device_id=peer_of(axis, step)[2], device_id_type=MESH)
    pl.semaphore_wait(barrier, len(steps))


def group_sum_kernel(dense_ref, out_ref, far, mixed, near, sems):
    tables, quarter, _ = out_ref.shape
    half = quarter // 2
    greet([(0, step) for step in range(1, 4)])
    mine, after, right = peer_of(0, 1)
    _, across, _ = peer_of(0, 2)
    _, before, left = peer_of(0, 3)
    ways = ((right, after, 0), (left, before, half))

    def share(t, owner, start):
        return dense_ref.at[t, pl.ds(pl.multiple_of(owner * quarter + start, half), half)]

    def hop(kind, t, way, src, dst):
        n = (kind * tables + t) * 2 + way
        copy = remote(src, dst, sems.at[0, n], sems.at[1, n], ways[way][0])
        copy.start()
        return copy

    firsts = [
        [hop(0, t, way, share(t, across, start), far.at[t, way]) for way, (_, _, start) in enumerate(ways)]
        for t in range(tables)
    ]
    others = [
        [
            hop(1, t, way, share(t, owner, half - start), near.at[t, way, pl.ds(half - start, half)])
            for way, (_, owner, start) in enumerate(ways)
        ]
        for t in range(tables)
    ]
    lasts = []
    for t in range(tables):
        for way, (_, owner, start) in enumerate(ways):
            firsts[t][way].wait_recv()
            kept = dense_ref[t, pl.ds(pl.multiple_of(owner * quarter + start, half), half), :]
            mixed[t, way] = (far[t, way].astype(F32) + kept.astype(F32)).astype(BF16)
        lasts.append(
            [hop(2, t, way, mixed.at[t, way], near.at[t, way, pl.ds(start, half)]) for way, (_, _, start) in enumerate(ways)]
        )
    for t in range(tables):
        for way in range(2):
            others[t][way].wait_recv()
            lasts[t][way].wait_recv()
        kept = dense_ref[t, pl.ds(pl.multiple_of(mine * quarter, quarter), quarter), :]
        out_ref[t] = kept.astype(F32) + near[t, 0].astype(F32) + near[t, 1].astype(F32)
    for copies in firsts + others + lasts:
        for copy in copies:
            copy.wait_send()


def group_sum(dense):
    tables, width, rows = dense.shape
    quarter = width // 4
    return pl.pallas_call(
        group_sum_kernel,
        out_shape=jax.ShapeDtypeStruct((tables, quarter, rows), F32),
        in_specs=[pl.BlockSpec(memory_space=pltpu.VMEM)],
        out_specs=pl.BlockSpec(memory_space=pltpu.VMEM),
        scratch_shapes=[
            pltpu.VMEM((tables, 2, quarter // 2, rows), BF16),
            pltpu.VMEM((tables, 2, quarter // 2, rows), BF16),
            pltpu.VMEM((tables, 2, quarter, rows), BF16),
            pltpu.SemaphoreType.DMA((2, 6 * tables)),
        ],
        compiler_params=pltpu.CompilerParams(collective_id=2, has_side_effects=True),
        cost_estimate=pl.CostEstimate(flops=10**6, bytes_accessed=60 * 10**6, transcendentals=0),
        name="group_sum",
    )(dense)


def on_device(shard_of, offsets, table, weight_one, gain_one, weight_two, gain_two, grad_out):
    sessions, length, _ = shard_of.shape
    width = table.shape[2]
    rows_dev = table.shape[1]
    rows = 3 * rows_dev
    item_count = sessions * length
    shards = lax.axis_size("table")
    groups = lax.axis_size("dp")
    slot_count = 8 * ((6 * item_count + 8 * shards - 1) // (8 * shards))
    place, asked, lists = make_index(
        jnp.transpose(shard_of, (2, 0, 1)), jnp.transpose(offsets, (2, 0, 1)), shards, slot_count, rows_dev
    )
    asked = asked.reshape(-1)
    got = exchange(asked, table.reshape(rows, width), shards, slot_count, 0, "rows_out")
    scale = 1.0 / math.sqrt(item_count * groups * shards)
    block_out, grad_embed, first_weights, second_weights, gains = block_pass(
        place.reshape(-1),
        got.reshape(-1, width),
        length,
        weight_one,
        gain_one,
        weight_two,
        gain_two,
        grad_out.reshape(item_count, width),
    )
    tiles = (-1, 8, width)
    arrived, totals = relay(
        lists.reshape(-1),
        grad_embed,
        shards,
        slot_count,
        first_weights.reshape(tiles),
        second_weights.reshape(tiles),
        gains,
        scale,
    )
    totals = totals.reshape(-1, width)
    dense = collect(asked, arrived.reshape(-1, width), rows, slot_count)
    table_grad = jnp.transpose(group_sum(dense), (0, 2, 1))
    block_out = block_out.reshape(sessions, length, width)
    return block_out, totals[:768], totals[768:1536], totals[1536], totals[1537], table_grad


def solution(mesh):
    placed = (
        P(("dp", "table"), None, None),
        P(("dp", "table"), None, None),
        P(None, "table", None),
        P(),
        P(),
        P(),
        P(),
        P(("dp", "table"), None, None),
    )
    return jax.shard_map(
        on_device,
        mesh=mesh,
        in_specs=placed,
        out_specs=(P(("dp", "table"), None, None), P(), P(), P(), P(), P(None, "table", "dp")),
        check_vma=False,
    )
```

```python
import functools
import math

import jax
import jax.numpy as jnp
from jax import lax
from jax.experimental import pallas as pl
from jax.experimental.pallas import tpu as pltpu
from jax.sharding import PartitionSpec as P

F32, BF16, I32 = jnp.float32, jnp.bfloat16, jnp.int32
MESH = pl.DeviceIdType.MESH
GELU_C = 0.7978845608028654
GELU_K = 0.044715
PITCH = 256
EDGE = 8
AXES = (("dp", 4, 1), ("table", 4, 16), ("table", 8, 2), ("table", 2, 1))


def gelu_parts(inputs):
    inner = GELU_C * (inputs + GELU_K * inputs * inputs * inputs)
    tangent = jnp.tanh(inner)
    output = 0.5 * inputs * (1.0 + tangent)
    slope = 0.5 * (1.0 + tangent) + 0.5 * inputs * (1.0 - tangent * tangent) * GELU_C * (
        1.0 + 3.0 * GELU_K * inputs * inputs
    )
    return (output, slope)


def index_kernel(cap, rows_dev, sh_ref, off_ref, place_ref, asked_ref, lists_ref, req_ref, item_ref, send, recv, list_send, list_recv):
    tables, sessions, length = sh_ref.shape
    shards = asked_ref.shape[0]
    me = lax.axis_index("table")
    barrier = pltpu.get_barrier_semaphore()

    def hello(step, _):
        pl.semaphore_signal(barrier, inc=1, device_id={"table": visit(step)}, device_id_type=MESH)
        return 0

    lax.fori_loop(1, shards, hello, 0)
    tri = (
        lax.broadcasted_iota(I32, (length, length), 0) < lax.broadcasted_iota(I32, (length, length), 1)
    ).astype(BF16)
    lane = lax.broadcasted_iota(I32, (1, length), 1)
    shard_id = lax.broadcasted_iota(I32, (shards, length), 0)
    slot_id = lax.broadcasted_iota(I32, (cap, length), 0)
    base = jnp.zeros((shards, 1), F32)
    listed = [jnp.zeros((shards, cap), F32) for _ in range(4)]
    dims = (((1,), (1,)), ((), ()))
    for t in range(tables):
        for s in range(sessions):
            sh = sh_ref[t, s : s + 1, :]
            code = off_ref[t, s : s + 1, :] + (t * rows_dev + EDGE)
            item = lane + (s * length + EDGE)
            hit = shard_id == sh
            hot = jnp.where(hit, 1.0, 0.0)
            hot16 = hot.astype(BF16)
            prefix = jnp.dot(hot16, tri, preferred_element_type=F32) + base
            rank = jnp.sum(jnp.where(hit, prefix, 0.0), axis=0, keepdims=True).astype(I32)
            base = base + jnp.sum(hot, axis=1, keepdims=True)
            place = sh * cap + rank
            place_ref[t * sessions + s, 0:1, :] = place[:, :128]
            place_ref[t * sessions + s, 1:2, 0 : length - 128] = place[:, 128:]
            here = slot_id == rank
            for n, digit in enumerate((code // 256, code % 256, item // 256, item % 256)):
                listed[n] += lax.dot_general(
                    hot16,
                    jnp.where(here, digit.astype(F32), 0.0).astype(BF16),
                    dims,
                    preferred_element_type=F32,
                )
    for ref, high, low in ((req_ref, listed[0], listed[1]), (item_ref, listed[2], listed[3])):
        codes = (high * 256.0 + low).astype(I32)
        ref[...] = jnp.zeros(ref.shape, I32)
        ref[:, 0, :] = codes[:, :128]
        ref[:, 1, 0 : cap - 128] = codes[:, 128:]
    pl.semaphore_wait(barrier, shards - 1)

    def ask(step, _):
        dest = visit(step)
        remote(req_ref.at[dest], asked_ref.at[me], send, recv, {"table": dest}).start()
        return 0

    lax.fori_loop(1, shards, ask, 0)
    asked_ref[me] = req_ref[me]
    ymine, zmine, cmine = spot()
    zsize, plane = lists_ref.shape[:2]

    def tell(step, _):
        z = lax.rem(zmine + step, zsize)
        for k in range(plane):
            source = item_ref.at[device_at(*plane_spot(k), z)]
            remote(source, lists_ref.at[zmine, k], list_send, list_recv, {"table": device_at(ymine, cmine, z)}).start()
        return 0

    lax.fori_loop(1, zsize, tell, 0)
    for k in range(plane):
        lists_ref[zmine, k] = item_ref[device_at(*plane_spot(k), zmine)]
    many = pl.ds(0, shards - 1)
    remote(req_ref.at[many], asked_ref.at[many], send, recv, {"table": visit(1)}).wait()
    many = item_ref.at[pl.ds(0, shards - plane)]
    remote(many, many, list_send, list_recv, {"table": visit(1)}).wait()


def make_index(sh, off, shards, cap, rows_dev):
    tables, sessions, _ = sh.shape
    block = jax.ShapeDtypeStruct((shards, 2, 128), I32)
    zsize = AXES[2][1]
    lists = jax.ShapeDtypeStruct((zsize, shards // zsize, 2, 128), I32)
    vmem = pl.BlockSpec(memory_space=pltpu.VMEM)
    return pl.pallas_call(
        functools.partial(index_kernel, cap, rows_dev),
        out_shape=(jax.ShapeDtypeStruct((tables * sessions, 2, 128), I32), block, lists),
        in_specs=[vmem] * 2,
        out_specs=[vmem] * 3,
        scratch_shapes=[pltpu.VMEM((shards, 2, 128), I32)] * 2 + [pltpu.SemaphoreType.DMA] * 4,
        compiler_params=pltpu.CompilerParams(collective_id=3, has_side_effects=True),
        cost_estimate=pl.CostEstimate(flops=10**9, bytes_accessed=10**6, transcendentals=0),
        name="index",
    )(sh, off)


def whole(shape):
    zeros = (0,) * len(shape)
    return pl.BlockSpec(shape, lambda b, i: zeros, pipeline_mode=pl.Buffered(1))


def widen(src, dst, rows, at=0):
    values = src[pl.ds(at, rows), :].astype(F32)
    dst[pl.ds(2 * at, rows, stride=2), :] = values[:, :128]
    dst[pl.ds(2 * at + 1, rows, stride=2), :] = values[:, 128:]


def pair(index):
    return pl.ds(pl.multiple_of(2 * index, 2), 2)


PAD = 8


def padded(values, length):
    zeros = jnp.zeros((PAD, values.shape[1]), F32)
    parts = []
    for start in range(0, values.shape[0], length):
        parts += [zeros, values[start : start + length]]
    return jnp.concatenate(parts, axis=0)


def unpadded(values, length):
    pitch = length + PAD
    return jnp.concatenate(
        [values[start + PAD : start + pitch] for start in range(0, values.shape[0], pitch)], axis=0
    )


def rolled(values, by):
    return [values.astype(BF16)] + [
        pltpu.roll(values, (k * by) % values.shape[0], 0).astype(BF16) for k in (1, 2)
    ]


def normalized(before):
    centred = before - jnp.mean(before, axis=-1, keepdims=True)
    inv_std = lax.rsqrt(jnp.mean(centred * centred, axis=-1, keepdims=True) + 1e-05)
    return centred * inv_std, inv_std


def forward(values, weight_ref, gain, spacing):
    width = values.shape[1]
    before = jnp.zeros(values.shape, F32)
    for k, tap in enumerate(rolled(values, spacing)):
        before += jnp.dot(tap, weight_ref[k * width : (k + 1) * width, :], preferred_element_type=F32)
    normal, inv_std = normalized(before)
    output, slope = gelu_parts(normal * gain)
    return output, normal, inv_std, slope


def backward(grad_output, values, saved, weight_ref, gain, spacing, weight_grad_ref):
    normal, inv_std, slope = saved
    width = values.shape[1]
    scaled = grad_output * slope
    gain_grad = jnp.sum(scaled * normal, axis=0, keepdims=True)
    back = scaled * gain
    before = inv_std * (
        back
        - jnp.mean(back, axis=-1, keepdims=True)
        - normal * jnp.mean(back * normal, axis=-1, keepdims=True)
    )
    grad_input = jnp.zeros(values.shape, F32)
    taken = values.astype(BF16)
    for k, tap in enumerate(rolled(before, -spacing)):
        rows = slice(k * width, (k + 1) * width)
        grad_input += lax.dot_general(
            tap, weight_ref[rows, :], (((1,), (1,)), ((), ())), preferred_element_type=F32
        )
        weight_grad_ref[rows, :] += lax.dot_general(
            taken, tap, (((0,), (0,)), ((), ())), preferred_element_type=F32
        )
    return grad_input, gain_grad


def block_kernel(
    length, place_ref, got_ref, w1_ref, g1_ref, w2_ref, g2_ref, top_ref,
    out_ref, grad_ref, dw1_ref, dw2_ref, gains_ref, wide, total,
):
    items, width = out_ref.shape
    slots = got_ref.shape[0]
    step = slots // 16

    @pl.loop(0, 16)
    def _(c):
        widen(got_ref, wide, step, pl.multiple_of(c * step, 16))

    sessions = items // length

    @pl.loop(0, items // 40)
    def _(g):
        session = g // (length // 40)
        at = session * PITCH + (g - session * (length // 40)) * 40
        to = pl.multiple_of(g * 80, 16)
        for k in range(40):
            a, b, c = [wide[pair(place_ref[t * sessions * PITCH + at + k]), :] for t in range(3)]
            total[pl.ds(to + 2 * k, 2), :] = a + b + c

    dw1_ref[...] = jnp.zeros(dw1_ref.shape, F32)
    dw2_ref[...] = jnp.zeros(dw2_ref.shape, F32)
    gains_ref[...] = jnp.zeros(gains_ref.shape, F32)
    chunk = 2 * length
    pitch = length + PAD
    row = lax.broadcasted_iota(I32, (2 * pitch, width), 0)
    real = ((row >= PAD) & (row < pitch)) | (row >= pitch + PAD)
    g1, g2 = g1_ref[...], g2_ref[...]

    @pl.loop(0, items // chunk)
    def _(c):
        at = pl.ds(pl.multiple_of(c * chunk, 16), chunk)
        embedded = jnp.concatenate(
            [total[pl.ds(2 * c * chunk + h, chunk, stride=2), :] for h in range(2)], axis=1
        )
        embedded = padded(embedded.astype(BF16).astype(F32), length)
        act_one, *saved_one = forward(embedded, w1_ref, g1, 1)
        hidden = jnp.where(real, act_one, 0.0).astype(BF16).astype(F32)
        act_two, *saved_two = forward(hidden, w2_ref, g2, 2)
        out_ref[at, :] = unpadded(embedded + act_two, length).astype(BF16)
        top = padded(top_ref[at, :].astype(F32), length)
        grad_hidden, gain_two = backward(top, hidden, saved_two, w2_ref, g2, 2, dw2_ref)
        grad_hidden = jnp.where(real, grad_hidden, 0.0)
        grad_inner, gain_one = backward(grad_hidden, embedded, saved_one, w1_ref, g1, 1, dw1_ref)
        grad_ref[at, :] = unpadded(top + grad_inner, length).astype(BF16)
        gains_ref[0:1, :] += gain_one
        gains_ref[1:2, :] += gain_two


def block_pass(place, got, length, weight_one, gain_one, weight_two, gain_two, grad_top):
    items, width = grad_top.shape
    operands = (got, weight_one, gain_one.reshape(1, -1), weight_two, gain_two.reshape(1, -1), grad_top)
    shapes = [
        ((items, width), BF16),
        ((items, width), BF16),
        (weight_one.shape, F32),
        (weight_two.shape, F32),
        ((8, width), F32),
    ]
    return pl.pallas_call(
        functools.partial(block_kernel, length),
        out_shape=[jax.ShapeDtypeStruct(*shape) for shape in shapes],
        grid_spec=pltpu.PrefetchScalarGridSpec(
            num_scalar_prefetch=1,
            grid=(1,),
            in_specs=[whole(operand.shape) for operand in operands],
            out_specs=[whole(shape) for shape, _ in shapes],
            scratch_shapes=[pltpu.VMEM((2 * got.shape[0], 128), F32), pltpu.VMEM((2 * items, 128), F32)],
        ),
        cost_estimate=pl.CostEstimate(flops=4 * 10**9, bytes_accessed=30 * 10**6, transcendentals=10**6),
        name="block_pass",
    )(place, *operands)


def collect_kernel(ways, cap, idx_ref, got_ref, out_ref, wide, *accs):
    b = pl.program_id(0)
    block = got_ref.shape[0]
    rows = accs[0].shape[0] // 2 - EDGE

    @pl.when(b == 0)
    def _():
        @pl.loop(0, rows // 256)
        def _(c):
            for acc in accs:
                acc[pl.ds(pl.multiple_of(2 * EDGE + c * 512, 16), 512), :] = jnp.zeros((512, 128), F32)

    widen(got_ref, wide, block)

    @pl.loop(0, block // cap)
    def _(g):
        at = pl.multiple_of(g * (2 * cap), 16)
        base = (b * (block // cap) + g) * PITCH
        for k in range(0, cap, ways):
            spots = [pair(idx_ref[base + k + j]) for j in range(ways)]
            olds = [accs[j][spots[j], :] for j in range(ways)]
            adds = [wide[pl.ds(at + 2 * (k + j), 2), :] for j in range(ways)]
            for j in range(ways):
                accs[j][spots[j], :] = olds[j] + adds[j]

    @pl.when(b == pl.num_programs(0) - 1)
    def _():
        @pl.loop(0, rows // 256)
        def _(c):
            per = out_ref.shape[2] // 256
            to = pl.ds(pl.multiple_of((c % per) * 256, 256), 256)
            for half in range(2):
                at = pl.ds(2 * EDGE + c * 512 + half, 256, stride=2)
                total = accs[0][at, :]
                for acc in accs[1:]:
                    total = total + acc[at, :]
                out_ref[c // per, 128 * half : 128 * half + 128, to] = total.T.astype(BF16)


def collect(idx, got, rows, cap, block=2432, ways=4):
    n, width = got.shape
    shape = (3, width, rows // 3)
    return pl.pallas_call(
        functools.partial(collect_kernel, ways, cap),
        out_shape=jax.ShapeDtypeStruct(shape, BF16),
        grid_spec=pltpu.PrefetchScalarGridSpec(
            num_scalar_prefetch=1,
            grid=(n // block,),
            in_specs=[pl.BlockSpec((block, width), lambda b, i: (b, 0))],
            out_specs=whole(shape),
            scratch_shapes=[pltpu.VMEM((2 * block, 128), F32)]
            + [pltpu.VMEM((2 * (rows + EDGE), 128), F32)] * ways,
        ),
        cost_estimate=pl.CostEstimate(flops=10**7, bytes_accessed=60 * 10**6, transcendentals=0),
        name="collect",
    )(idx, got)


def peer_of(axis, step):
    name, size, stride = AXES[axis]
    index = lax.axis_index(name)
    mine = lax.rem(lax.div(index, stride), size)
    other = lax.rem(mine + step, size)
    return mine, other, {name: index + (other - mine) * stride}


def visit(step):
    (_, ysize, ystride), (_, zsize, zstride), (_, csize, _) = AXES[1:]
    me = lax.axis_index("table")
    y, z, c = lax.div(me, ystride), lax.rem(lax.div(me, zstride), zsize), lax.rem(me, csize)
    turn = lax.rem(step, zsize)
    half = lax.div(turn + 1, 2)
    away = jnp.where(lax.rem(turn, 2) == 1, half, zsize - half)
    y = lax.rem(y + lax.rem(lax.div(step, zsize), ysize), ysize)
    z = lax.rem(z + away, zsize)
    c = lax.rem(c + lax.div(step, zsize * ysize), csize)
    return y * ystride + z * zstride + c


def spot():
    me = lax.axis_index("table")
    (_, _, ystride), (_, zsize, zstride), (_, csize, _) = AXES[1:]
    return lax.div(me, ystride), lax.rem(lax.div(me, zstride), zsize), lax.rem(me, csize)


def device_at(y, c, z):
    return y * AXES[1][2] + z * AXES[2][2] + c


def plane_spot(k):
    return k // AXES[3][1], k % AXES[3][1]


def remote(src, dst, send, recv, device):
    return pltpu.make_async_remote_copy(
        src_ref=src, dst_ref=dst, send_sem=send, recv_sem=recv, device_id=device, device_id_type=MESH
    )


def exchange_kernel(idx_ref, table_ref, got_ref, wide, stage, held, own_sem, send, recv):
    shards, cap, width = held.shape
    rows = table_ref.shape[0]
    me = lax.axis_index("table")
    total = shards - 1
    barrier = pltpu.get_barrier_semaphore()

    def hello(step, _):
        pl.semaphore_signal(barrier, inc=1, device_id={"table": visit(step)}, device_id_type=MESH)
        return 0

    lax.fori_loop(1, shards, hello, 0)

    def widened(c, _):
        at = pl.ds(pl.multiple_of(c * 64, 64), 64)
        wide[pl.ds(pl.multiple_of(EDGE + c * 64, EDGE), 64), :] = table_ref[at, :].astype(F32)
        return 0

    wide[0:EDGE, :] = jnp.zeros((EDGE, width), F32)
    lax.fori_loop(0, rows // 64, widened, 0)

    def gather(step):
        dest = visit(step)
        for k in range(0, cap, 8):
            rows8 = [wide[pl.ds(idx_ref[dest * PITCH + k + j], 1), :] for j in range(8)]
            stage[k : k + 8, :] = jnp.concatenate(rows8, axis=0)
        held[step] = stage[...].astype(BF16)

    def post(step):
        remote(held.at[step], got_ref.at[me], send, recv, {"table": visit(step)}).start()

    gather(1)
    pl.semaphore_wait(barrier, total)

    def go(step, _):
        gather(step)
        post(step - 1)
        return 0

    lax.fori_loop(2, shards, go, 0)
    post(total)
    gather(0)
    own = pltpu.make_async_copy(held.at[0], got_ref.at[me], own_sem)
    own.start()
    own.wait()
    many = pl.ds(0, total)
    remote(held.at[many], got_ref.at[many], send, recv, {"table": visit(1)}).wait()


def exchange(idx, table, shards, cap, collective_id, name):
    rows, width = table.shape
    return pl.pallas_call(
        exchange_kernel,
        out_shape=jax.ShapeDtypeStruct((shards, cap, width), BF16),
        in_specs=[pl.BlockSpec(memory_space=pltpu.SMEM), pl.BlockSpec(memory_space=pltpu.VMEM)],
        out_specs=pl.BlockSpec(memory_space=pl.ANY),
        scratch_shapes=[
            pltpu.VMEM((rows + EDGE, width), F32),
            pltpu.VMEM((cap, width), F32),
            pltpu.VMEM((shards, cap, width), BF16),
            pltpu.SemaphoreType.DMA,
            pltpu.SemaphoreType.DMA,
            pltpu.SemaphoreType.DMA,
        ],
        compiler_params=pltpu.CompilerParams(collective_id=collective_id, has_side_effects=True),
        cost_estimate=pl.CostEstimate(flops=10**7, bytes_accessed=10**8, transcendentals=0),
        name=name,
    )(idx, table)


def relay_kernel(
    scale, idx_ref, table_ref, w1_ref, w2_ref, gains_ref, got_ref, out_ref,
    blocks, wide, stage, held, own_sem, ring_send, ring_recv, send, recv,
    part, r0, s0, r1, s1, r2, a2, a1, *sems,
):
    zsize, rows, width = blocks.shape
    shards, cap, _ = held.shape
    plane = shards // zsize
    me = lax.axis_index("table")
    ymine, zmine, cmine = spot()
    parts = [(w1_ref, w1_ref.shape[0]), (w2_ref, w2_ref.shape[0]), (gains_ref, 1)]
    ysize, zcsize = part.shape[1:3]
    block = 0
    for ref, count in parts:
        done = 0
        while done < count:
            many = min(count - done, zcsize - block % zcsize)
            first = block % zcsize
            row = ref[...][None] if ref is gains_ref else ref[done : done + many]
            part[block // (ysize * zcsize), block // zcsize % ysize, first : first + many] = row
            done, block = done + many, block + many
    while block < part.shape[0] * ysize * zcsize:
        many = zcsize - block % zcsize
        empty = jnp.zeros((many,) + part.shape[3:], F32)
        part[block // (ysize * zcsize), block // zcsize % ysize, block % zcsize :] = empty
        block += many
    zcmine = lax.rem(me, zcsize)
    xmine = peer_of(0, 1)[0]
    xpeers = [peer_of(0, step)[1:] for step in range(1, AXES[0][1])]
    ypeers = [lax.rem(ymine + step, ysize) for step in range(1, ysize)]
    ypeers = [(other, {"table": other * zcsize + zcmine}) for other in ypeers]
    zcpeers = [lax.rem(zcmine + step, zcsize) for step in range(1, zcsize)]
    zcpeers = [(other, {"table": ymine * zcsize + other}) for other in zcpeers]

    def fan(stage, peers, src, dst):
        send_sem, recv_sem = sems[2 * stage : 2 * stage + 2]
        copies = [
            remote(src(other), dst(n), send_sem.at[n], recv_sem.at[n], device)
            for n, (other, device) in enumerate(peers)
        ]
        for copy in copies:
            copy.start()
        return copies

    def landed(copies):
        for copy in copies:
            copy.wait_recv()

    barrier = pltpu.get_barrier_semaphore()
    others = []
    for dy in range(1, ysize):
        for dc in range(AXES[3][1]):
            y, c = lax.rem(ymine + dy, ysize), lax.rem(cmine + dc, AXES[3][1])
            others.append({"table": device_at(y, c, zmine)})
    known = [device for _, device in xpeers + zcpeers] + others
    for device in known:
        pl.semaphore_signal(barrier, inc=1, device_id=device, device_id_type=MESH)
    wide[0:EDGE, :] = jnp.zeros((EDGE, width), F32)
    pl.semaphore_wait(barrier, len(known))
    right = {"table": device_at(ymine, cmine, lax.rem(zmine + 1, zsize))}
    left = {"table": device_at(ymine, cmine, lax.rem(zmine + zsize - 1, zsize))}
    far = zsize // 2
    half = rows // 2

    def ring(way, hop):
        source = lax.rem(zmine + (zsize - hop if way == 0 else hop), zsize)
        src, dst = table_ref if hop == 0 else blocks.at[source], blocks.at[source]
        if hop == far - 1:
            at = pl.ds(way * half, half)
            src, dst = src.at[at], dst.at[at]
        return remote(src, dst, ring_send.at[way, hop], ring_recv.at[way, hop], right if way == 0 else left)

    copies = {(way, hop): ring(way, hop) for way in range(2) for hop in range(far)}
    flights = [fan(0, xpeers, lambda other: part.at[other], lambda n: r0.at[n])]
    for way in range(2):
        copies[way, 0].start()

    def serve(number, source, rows_ref):
        def widened(c, _):
            at = pl.ds(pl.multiple_of(c * 64, 64), 64)
            wide[pl.ds(pl.multiple_of(EDGE + c * 64, EDGE), 64), :] = rows_ref[at, :].astype(F32)
            return 0

        lax.fori_loop(0, rows // 64, widened, 0)
        origin = device_at(ymine, cmine, source)

        def turned(step):
            y, c = plane_spot(step)
            return lax.rem(ymine + y, ysize), lax.rem(cmine + c, AXES[3][1])

        def gather(step):
            y, c = turned(step)
            base = (source * plane + y * AXES[3][1] + c) * PITCH
            for k in range(0, cap, 8):
                rows8 = [wide[pl.ds(idx_ref[base + k + j], 1), :] for j in range(8)]
                stage[k : k + 8, :] = jnp.concatenate(rows8, axis=0)
            held[number * plane + step] = stage[...].astype(BF16)

        def post(step):
            y, c = turned(step)
            remote(
                held.at[number * plane + step], got_ref.at[origin], send, recv, {"table": device_at(y, c, zmine)}
            ).start()

        def go(step, _):
            gather(step)
            post(step - 1)
            return 0

        gather(1)
        lax.fori_loop(2, plane, go, 0)
        post(plane - 1)
        gather(0)
        own = pltpu.make_async_copy(held.at[number * plane], got_ref.at[origin], own_sem.at[number])
        own.start()
        return own

    def sum_stage(stage_number):
        landed(flights[-1])
        if stage_number == 1:
            s0[...] = sum([r0[n] for n in range(len(xpeers))], part[xmine])
            flights.append(fan(1, ypeers, lambda other: s0.at[other], lambda n: r1.at[n]))
        elif stage_number == 2:
            s1[...] = sum([r1[n] for n in range(len(ypeers))], s0[ymine])
            flights.append(fan(2, zcpeers, lambda other: s1.at[other], lambda n: r2.at[n]))
        elif stage_number == 3:
            a2[zcmine] = sum([r2[n] for n in range(len(zcpeers))], s1[zcmine]) * scale
            flights.append(fan(3, zcpeers, lambda _: a2.at[zcmine], lambda _: a2.at[zcmine]))
        elif stage_number == 4:
            flights.append(fan(4, ypeers, lambda _: a2, lambda _: a1.at[ymine]))
            a1[ymine] = a2[...]
        elif stage_number == 5:
            flights.append(fan(5, xpeers, lambda _: a1, lambda _: out_ref.at[xmine]))
            out_ref[xmine] = a1[...]

    locals_ = [serve(0, zmine, table_ref)]
    for hop in range(1, far + 1):
        sources = [lax.rem(zmine + (zsize - hop if way == 0 else hop), zsize) for way in range(2)]
        for way in range(2):
            copies[way, hop - 1].wait_recv()
            if hop < far:
                copies[way, hop].start()
        if hop > 1:
            sum_stage(hop)
        for way in range(2 if hop < far else 1):
            locals_.append(serve(2 * hop - 1 + way, sources[way], blocks.at[sources[way]]))
        if hop == 1:
            sum_stage(1)
    for stage_number in range(far + 1, 6):
        sum_stage(stage_number)
    for copy in copies.values():
        copy.wait_send()
    for copy in locals_:
        copy.wait()
    many = pl.ds(0, shards - zsize)
    remote(held.at[many], got_ref.at[many], send, recv, right).wait()
    landed(flights[-1])
    for flight in flights:
        for copy in flight:
            copy.wait_send()


def relay(idx, table, shards, cap, w1, w2, gains, scale):
    rows, width = table.shape
    (xsize, ysize, zsize), zcsize = [AXES[n][1] for n in range(3)], AXES[1][2]
    tile = w1.shape[1:]
    line, plane = (zcsize,) + tile, (ysize, zcsize) + tile
    shapes = [(xsize,) + plane, (xsize - 1,) + plane, plane, (ysize - 1,) + line, line]
    shapes += [(zcsize - 1,) + tile, line, plane]
    dma = pltpu.SemaphoreType.DMA
    scratch = [
        pltpu.VMEM((zsize, rows, width), BF16),
        pltpu.VMEM((rows + EDGE, width), F32),
        pltpu.VMEM((cap, width), F32),
        pltpu.VMEM((shards, cap, width), BF16),
        dma((zsize,)),
        dma((2, zsize // 2)),
        dma((2, zsize // 2)),
        dma,
        dma,
    ]
    scratch += [pltpu.VMEM(shape, F32) for shape in shapes]
    for size in (xsize, ysize, zcsize, zcsize, ysize, xsize):
        scratch += [dma((size - 1,))] * 2
    vmem = pl.BlockSpec(memory_space=pltpu.VMEM)
    return pl.pallas_call(
        functools.partial(relay_kernel, scale),
        out_shape=[
            jax.ShapeDtypeStruct((shards, cap, width), BF16),
            jax.ShapeDtypeStruct((xsize,) + plane, F32),
        ],
        in_specs=[pl.BlockSpec(memory_space=pltpu.SMEM)] + [vmem] * 4,
        out_specs=[pl.BlockSpec(memory_space=pl.ANY), vmem],
        scratch_shapes=scratch,
        compiler_params=pltpu.CompilerParams(collective_id=1, has_side_effects=True),
        cost_estimate=pl.CostEstimate(flops=10**7, bytes_accessed=10**8, transcendentals=0),
        name="grads_out",
    )(idx, table, w1, w2, gains)


def greet(steps):
    barrier = pltpu.get_barrier_semaphore()
    for axis, step in steps:
        pl.semaphore_signal(barrier, inc=1, device_id=peer_of(axis, step)[2], device_id_type=MESH)
    pl.semaphore_wait(barrier, len(steps))


def group_sum_kernel(dense_ref, out_ref, far, mixed, near, sems):
    tables, quarter, _ = out_ref.shape
    half = quarter // 2
    greet([(0, step) for step in range(1, 4)])
    mine, after, right = peer_of(0, 1)
    _, across, _ = peer_of(0, 2)
    _, before, left = peer_of(0, 3)
    ways = ((right, after, 0), (left, before, half))

    def share(t, owner, start):
        return dense_ref.at[t, pl.ds(pl.multiple_of(owner * quarter + start, half), half)]

    def hop(kind, t, way, src, dst):
        n = (kind * tables + t) * 2 + way
        copy = remote(src, dst, sems.at[0, n], sems.at[1, n], ways[way][0])
        copy.start()
        return copy

    firsts = [
        [hop(0, t, way, share(t, across, start), far.at[t, way]) for way, (_, _, start) in enumerate(ways)]
        for t in range(tables)
    ]
    others = [
        [
            hop(1, t, way, share(t, owner, half - start), near.at[t, way, pl.ds(half - start, half)])
            for way, (_, owner, start) in enumerate(ways)
        ]
        for t in range(tables)
    ]
    lasts = []
    for t in range(tables):
        for way, (_, owner, start) in enumerate(ways):
            firsts[t][way].wait_recv()
            kept = dense_ref[t, pl.ds(pl.multiple_of(owner * quarter + start, half), half), :]
            mixed[t, way] = (far[t, way].astype(F32) + kept.astype(F32)).astype(BF16)
        lasts.append(
            [hop(2, t, way, mixed.at[t, way], near.at[t, way, pl.ds(start, half)]) for way, (_, _, start) in enumerate(ways)]
        )
    for t in range(tables):
        for way in range(2):
            others[t][way].wait_recv()
            lasts[t][way].wait_recv()
        kept = dense_ref[t, pl.ds(pl.multiple_of(mine * quarter, quarter), quarter), :]
        out_ref[t] = kept.astype(F32) + near[t, 0].astype(F32) + near[t, 1].astype(F32)
    for copies in firsts + others + lasts:
        for copy in copies:
            copy.wait_send()


def group_sum(dense):
    tables, width, rows = dense.shape
    quarter = width // 4
    return pl.pallas_call(
        group_sum_kernel,
        out_shape=jax.ShapeDtypeStruct((tables, quarter, rows), F32),
        in_specs=[pl.BlockSpec(memory_space=pltpu.VMEM)],
        out_specs=pl.BlockSpec(memory_space=pltpu.VMEM),
        scratch_shapes=[
            pltpu.VMEM((tables, 2, quarter // 2, rows), BF16),
            pltpu.VMEM((tables, 2, quarter // 2, rows), BF16),
            pltpu.VMEM((tables, 2, quarter, rows), BF16),
            pltpu.SemaphoreType.DMA((2, 6 * tables)),
        ],
        compiler_params=pltpu.CompilerParams(collective_id=2, has_side_effects=True),
        cost_estimate=pl.CostEstimate(flops=10**6, bytes_accessed=60 * 10**6, transcendentals=0),
        name="group_sum",
    )(dense)


def on_device(shard_of, offsets, table, weight_one, gain_one, weight_two, gain_two, grad_out):
    sessions, length, _ = shard_of.shape
    width = table.shape[2]
    rows_dev = table.shape[1]
    rows = 3 * rows_dev
    item_count = sessions * length
    shards = lax.axis_size("table")
    groups = lax.axis_size("dp")
    slot_count = 8 * ((6 * item_count + 8 * shards - 1) // (8 * shards))
    place, asked, lists = make_index(
        jnp.transpose(shard_of, (2, 0, 1)), jnp.transpose(offsets, (2, 0, 1)), shards, slot_count, rows_dev
    )
    asked = asked.reshape(-1)
    got = exchange(asked, table.reshape(rows, width), shards, slot_count, 0, "rows_out")
    scale = 1.0 / math.sqrt(item_count * groups * shards)
    block_out, grad_embed, first_weights, second_weights, gains = block_pass(
        place.reshape(-1),
        got.reshape(-1, width),
        length,
        weight_one,
        gain_one,
        weight_two,
        gain_two,
        grad_out.reshape(item_count, width),
    )
    tiles = (-1, 8, width)
    arrived, totals = relay(
        lists.reshape(-1),
        grad_embed,
        shards,
        slot_count,
        first_weights.reshape(tiles),
        second_weights.reshape(tiles),
        gains,
        scale,
    )
    totals = totals.reshape(-1, width)
    dense = collect(asked, arrived.reshape(-1, width), rows, slot_count)
    table_grad = jnp.transpose(group_sum(dense), (0, 2, 1))
    block_out = block_out.reshape(sessions, length, width)
    return block_out, totals[:768], totals[768:1536], totals[1536], totals[1537], table_grad


def solution(mesh):
    placed = (
        P(("dp", "table"), None, None),
        P(("dp", "table"), None, None),
        P(None, "table", None),
        P(),
        P(),
        P(),
        P(),
        P(("dp", "table"), None, None),
    )
    return jax.shard_map(
        on_device,
        mesh=mesh,
        in_specs=placed,
        out_specs=(P(("dp", "table"), None, None), P(), P(), P(), P(), P(None, "table", "dp")),
        check_vma=False,
    )
```
